128 devices in a mesh: layer: 2 (over core), row: 64 (over z, y, x).
Axes of the slice: x: 4, y: 4, z: 4, core: 2. Of those that a mesh axis runs over, the one named last changes fastest.
Arguments:
- sources: bfloat16 [2, 4608, 512], P('layer', 'row'), may hold values from -2 to 2
- green_down: bfloat16 [2, 4608, 4608], P('layer', 'row')
- green_up: bfloat16 [2, 4608, 4608], P('layer', 'row')
- material: int32 [8, 4608], P('layer', 'row'), may hold values 0 or 1
- pml_cells: int32 [1], replicated, may hold values from 4 to 39
Outputs:
- residual: bfloat16 [8, 4608, 512], P('layer', 'row')
The draws below stay inside these ranges and needn't reach their ends.
All inputs are finite; a program needn't handle non-finite values. No bound on the sum of `material` on one device may be relied on, other than what follows from the above.
Results may differ from the reference program's by a relative error of at most 0.005.
Values may be sent and summed in bfloat16 or wider, within the bound.
A program may use at most 64 MiB of HBM per device.

```python
import jax
import jax.numpy as jnp
from jax import lax

M = 4608
K = 4
LAYERS = 2
SRC = 512
ZS = 8


def green_matrix(key):
    key_diag, key_rest = jax.random.split(key)
    diag = jax.random.uniform(key_diag, (LAYERS, 1, 1), jnp.float32, 0.8, 0.93)
    rest = jax.random.normal(key_rest, (LAYERS, M, M), jnp.float32)
    eye = jnp.eye(M, dtype=jnp.float32)[None]
    return (diag * eye + 0.3 * rest / jnp.sqrt(float(M))).astype(jnp.bfloat16)


def draw_green_down(key, part):
    return green_matrix(jax.random.fold_in(key, 11))


def draw_green_up(key, part):
    return green_matrix(jax.random.fold_in(key, 23))


def plant(values, rng, least, high):
    shape = values.shape
    spot = [jax.random.randint(jax.random.fold_in(rng, axis), (), 0, shape[axis]) for axis in range(len(shape))]
    values = values.at[tuple(spot)].set(least)
    longest = shape.index(max(shape))
    spot[longest] = (spot[longest] + 1) % shape[longest]
    return values.at[tuple(spot)].set(high)


def steps_of(rng, shape, shards, least, largest):
    def one(axis_at, blocks):
        heights = jax.random.uniform(jax.random.fold_in(jax.random.fold_in(rng, 6), axis_at), (blocks,), jnp.float32, least / len(shards), largest / len(shards))
        return jnp.repeat(jnp.exp(heights), shape[axis_at] // blocks).reshape((-1,) + (1,) * (len(shape) - axis_at - 1))

    loudness = one(*shards[0])
    for cut in shards[1:]:
        loudness = loudness * one(*cut)
    return loudness


def noise(stream_key, extent, deviation, limit, cuts=(), kind=jnp.bfloat16):
    entries = jax.random.normal(stream_key, extent, jnp.float32) * deviation
    if len(cuts) > 0:
        entries = steps_of(stream_key, extent, cuts, -0.22, 0.18) * entries
    return jnp.clip(entries, min=-limit, max=limit).astype(kind)


def setup_inputs(seed: int = 0) -> dict:
    arg_keys = jax.random.split(jax.random.key(seed), 6)
    return {
        "sources": noise(arg_keys[0], (LAYERS, M, SRC), 0.3, 2.0, ((0, 2), (1, 64))),
        "green_down": draw_green_down(jax.random.fold_in(arg_keys[5], 71), 0),
        "green_up": draw_green_up(jax.random.fold_in(arg_keys[5], 71), 0),
        "material": plant((jax.random.randint(arg_keys[3], (ZS, M), 0, 2) < 1).astype(jnp.int32), jax.random.fold_in(arg_keys[3], 1), 0, 1),
        "pml_cells": jax.random.randint(arg_keys[4], (1,), 4, 40).astype(jnp.int32),
    }


def sweep(green, sources, reverse):
    def advance(carry, item):
        matrix, source = item
        entry = (source.astype(jnp.float32) + carry.astype(jnp.float32)).astype(jnp.bfloat16)
        result = jnp.dot(matrix.astype(jnp.float32), entry.astype(jnp.float32), precision=lax.Precision.HIGHEST).astype(jnp.bfloat16)
        return result, result
    start = jnp.zeros((M, SRC), jnp.bfloat16)
    unused, traces = lax.scan(advance, start, (green, sources), reverse=reverse)
    return traces


def ramp(index, count, thick):
    dist = jnp.minimum(index, count - 1 - index).astype(jnp.float32)
    return jnp.maximum(thick - dist, 0.0) / thick


def reference(sources, green_down, green_up, material, pml_cells):
    down = sweep(green_down, sources, False)
    up = sweep(green_up, sources, True)
    wave = sources.astype(jnp.float32) + down.astype(jnp.float32) + up.astype(jnp.float32)
    factor = (K - jnp.arange(K, dtype=jnp.float32)) / K
    slab = (wave[:, None, :, :] * factor[None, :, None, None]).reshape(ZS, M, SRC)
    thick = pml_cells[0].astype(jnp.float32)
    ramp_z = ramp(jnp.arange(ZS, dtype=jnp.int32), ZS, thick)
    ramp_m = ramp(jnp.arange(M, dtype=jnp.int32), M, thick)
    sigma = 3.0 * (ramp_z[:, None] * ramp_z[:, None] + ramp_m[None, :] * ramp_m[None, :])
    kappa = 1.0 + 1.5 * material.astype(jnp.float32)
    padded = jnp.pad(slab, ((1, 1), (1, 1), (0, 0)))
    beside = padded[2:, 1:-1] + padded[:-2, 1:-1] + padded[1:-1, 2:] + padded[1:-1, :-2]
    result = kappa[:, :, None] * ((4.0 + sigma)[:, :, None] * slab - beside)
    return result.astype(jnp.bfloat16)
```

```python
import functools

import jax
import jax.numpy as jnp
from jax import lax
from jax.experimental import pallas as pl
from jax.experimental.pallas import tpu as pltpu
from jax.sharding import PartitionSpec as P

MESH = pl.DeviceIdType.MESH
F32, BF16 = jnp.float32, jnp.bfloat16
N = 4
LANES = 128


def device(layer, z, y, x):
    return (layer, (z * N + y) * N + x)


def kernel(
    src, gd, gu, mat, pml, out,
    green, xin, res, fin, hal, own88, other, wave, kc, kf, mt,
    bulk_s, bulk_r, fwd_s, fwd_r, src_s, src_r, x_s, x_r, fin_s, fin_r,
    hal_s, hal_r, edge_s, edge_r, loc,
):
    layer = lax.axis_index("layer")
    row = lax.axis_index("row")
    z, y, x = row // (N * N), (row // N) % N, row % N
    group = z * N + y
    rows = src.shape[1]
    chunk = N * N * rows
    sweep = x // 2
    sib = 1 - layer
    mine = (layer + sweep) % 2

    def shift(a, d):
        return lax.rem(a + d, N)

    def remote(s, d, ss, rs, to):
        return pltpu.make_async_remote_copy(
            src_ref=s, dst_ref=d, send_sem=ss, recv_sem=rs, device_id=to, device_id_type=MESH
        )

    greet = [device(sib, z, y, x)]
    for d in (1, 2, 3):
        greet += [device(layer, z, y, shift(x, d)), device(sib, z, y, shift(x, d))]
        greet += [device(layer, z, shift(y, d), x), device(layer, shift(z, d), y, x)]
    barrier = pltpu.get_barrier_semaphore()
    for to in greet:
        pl.semaphore_signal(barrier, inc=1, device_id=to, device_id_type=MESH)

    def part_of_source(to_x, to_layer):
        quarter = 2 * lax.rem(to_x, 2) + to_layer
        return src.at[0, :, pl.ds(pl.multiple_of(quarter * LANES, LANES), LANES)]

    own_src = pltpu.make_async_copy(part_of_source(x, layer), xin.at[mine, z, y, x], loc.at[0])
    own_src.start()
    own_88 = pltpu.make_async_copy(src.at[0], own88.at[pl.ds(8, rows)], loc.at[1])
    own_88.start()
    own_green = []
    for c in range(N):
        cols = pl.ds(pl.multiple_of(shift(z, c) * chunk, LANES), chunk)
        to = green.at[mine, shift(z, c), x]
        for s, ref in ((0, gd), (1, gu)):
            @pl.when(sweep == s)
            def _(ref=ref, cols=cols, to=to, c=c):
                pltpu.make_async_copy(ref.at[0, :, cols], to, loc.at[2 + c]).start()
        own_green.append(pltpu.make_async_copy(gd.at[0, :, cols], to, loc.at[2 + c]))

    pl.semaphore_wait(barrier, len(greet))

    def source_copy(dx, dl):
        to_x = shift(x, dx)
        to_l = layer if dl == 0 else sib
        rnd = (layer + to_x // 2) % 2
        return remote(
            part_of_source(to_x, to_l), xin.at[rnd, z, y, x], src_s.at[dl, dx], src_r.at[dl, dx],
            device(to_l, z, y, to_x),
        )

    pairs = [(dx, dl) for dx in (2, 1, 3, 0) for dl in (0, 1) if (dx, dl) != (0, 0)]
    source_copies = {p: source_copy(*p) for p in pairs}
    for p in pairs:
        source_copies[p].start()

    def green_copy(dx, c, ref, s):
        cols = pl.ds(pl.multiple_of(shift(z, c) * chunk, LANES), chunk)
        rnd = (layer + s) % 2
        return remote(
            ref.at[0, :, cols], green.at[rnd, shift(z, c), x], bulk_s.at[dx, c], bulk_r.at[dx, c],
            device(layer, z, y, shift(x, dx)),
        )

    order = (0, 1, 3, 2)
    for first in (True, False):
        for s, ref in ((0, gd), (1, gu)):
            now = (layer == s) if first else (layer != s)
            for dx in (2, 1, 3):
                @pl.when(jnp.logical_and(now, shift(x, dx) // 2 == s))
                def _(s=s, ref=ref, dx=dx):
                    for c in order:
                        green_copy(dx, c, ref, s).start()

    other_copy = remote(src.at[0], other, edge_s.at[2], edge_r.at[2], device(sib, z, y, x))
    other_copy.start()

    rows_at = lax.broadcasted_iota(jnp.int32, (rows, LANES), 0) + row * rows
    thick = jnp.full((rows, LANES), pml[0].astype(F32))
    total = rows * N * N * N

    def ramp(index, count):
        dist = jnp.minimum(index, count - 1 - index).astype(F32)
        return jnp.maximum(thick - dist, 0.0) / thick

    ramp_m = ramp(rows_at, total)
    mt[...] = jnp.zeros_like(mt)
    mt[0:4, 0:rows] = 1.0 + 1.5 * mat[...].astype(F32)
    kappa = mt[...].T
    for k in range(4):
        ramp_z = ramp(jnp.full((rows, LANES), layer * 4 + k, jnp.int32), 8)
        sigma = 3.0 * (ramp_z * ramp_z + ramp_m * ramp_m)
        f = (4 - k) / 4
        around = (0 if k == 0 else (5 - k) / 4) + (0 if k == 3 else (3 - k) / 4)
        kap = jnp.broadcast_to(kappa[0:rows, k : k + 1], (rows, LANES))
        kc[k] = kap * (f * (4.0 + sigma) - around)
        kf[k] = kap * f
    res[:, 0:8] = jnp.zeros((2, 8, LANES), BF16)
    res[:, 4 * rows + 8 :] = jnp.zeros((2, 8, LANES), BF16)

    halves = (pl.ds(0, 2), pl.ds(2, 2))

    def plane_copy(rnd, part, from_z, from_y, sz, sy, to_z, to_y):
        at = xin.at[rnd, from_z, from_y, halves[part]]
        return remote(
            at, at, x_s.at[rnd, part, sz, sy], x_r.at[rnd, part, sz, sy],
            device(layer, to_z, to_y, x),
        )

    def first_stage(rnd):
        done = []
        for d in (2, 1, 3):
            done.append(plane_copy(rnd, 0, z, y, 0, d, z, shift(y, d)))
            done.append(plane_copy(rnd, 1, z, y, d, 0, shift(z, d), y))
        for d in (2, 1, 3):
            done.append(plane_copy(rnd, 0, z, y, d, 0, shift(z, d), y))
            done.append(plane_copy(rnd, 1, z, y, 0, d, z, shift(y, d)))
        for c in done:
            c.start()
        return done

    def arrival(rnd, part, sz, sy):
        from_z, from_y = shift(z, N - sz), shift(y, N - sy)
        at = xin.at[rnd, from_z, from_y, halves[part]]
        return remote(
            at, at, x_s.at[rnd, part, sz, sy], x_r.at[rnd, part, sz, sy], device(layer, z, y, x)
        )

    def second_stage(rnd):
        done = []
        for d in (1, 3, 2):
            arrival(rnd, 0, 0, d).wait_recv()
            for q in (2, 1, 3):
                done.append(plane_copy(rnd, 0, z, shift(y, N - d), q, d, shift(z, q), y))
                done[-1].start()
            arrival(rnd, 1, d, 0).wait_recv()
            for q in (2, 1, 3):
                done.append(plane_copy(rnd, 1, shift(z, N - d), y, d, q, z, shift(y, q)))
                done[-1].start()
        return done

    def wait_plane(rnd, sz):
        for sy in (0, 1, 3, 2):
            for part in (0, 1):
                if (sz, sy) != (0, 0) and not (part == 0 and sz == 0) and not (part == 1 and sy == 0):
                    arrival(rnd, part, sz, sy).wait_recv()

    def forward(dx, c):
        at = green.at[mine, shift(z, c), shift(x, N - dx)]
        return remote(at, at, fwd_s.at[dx, c], fwd_r.at[dx, c], device(sib, z, y, x))

    def from_sibling(dx, c):
        at = green.at[1 - mine, shift(z, c), shift(x, N - dx)]
        return remote(at, at, fwd_s.at[dx, c], fwd_r.at[dx, c], device(sib, z, y, x))

    def wait_green(rnd, c):
        @pl.when(mine == rnd)
        def _():
            for dx in (0, 1, 3, 2):
                if dx == 0:
                    own_green[c].wait()
                else:
                    green_copy(dx, c, gd, 0).wait_recv()
                forward(dx, c).start()

        @pl.when(mine != rnd)
        def _():
            for dx in (0, 1, 3, 2):
                from_sibling(dx, c).wait_recv()

    def product(rnd):
        acc = None
        for c in order:
            wait_green(rnd, c)
            wait_plane(rnd, (N - c) % N)
            g = green[rnd, shift(z, c)].reshape(N * rows, chunk)
            v = xin[rnd, shift(z, c)].reshape(chunk, LANES)
            term = jnp.dot(g, v, preferred_element_type=F32)
            acc = term if acc is None else acc + term
        return acc.astype(BF16)

    def share(rnd):
        at_layer = sweep if rnd == 0 else 1 - sweep
        quarter = 2 * lax.rem(x, 2) + layer
        done = []
        for dx in (2, 1, 3, 0):
            to_x = shift(x, dx)
            at = res.at[rnd, pl.ds(pl.multiple_of(to_x * rows, 8), rows + 16)]
            to = fin.at[sweep, at_layer, quarter]
            for dl in (0, 1):
                if (dx, dl) == (0, 0):
                    done.append(pltpu.make_async_copy(at, to, loc.at[6 + rnd]))
                else:
                    done.append(remote(
                        at, to, fin_s.at[rnd, dl, dx], fin_r.at[rnd, dl, dx],
                        device(layer if dl == 0 else sib, z, y, to_x),
                    ))
        to = hal.at[sweep, quarter]
        up = remote(
            res.at[rnd, pl.ds(N * rows, 8)], to, hal_s.at[rnd, 0], hal_r.at[x, layer],
            (at_layer, lax.rem((group + 1) * N, N * N * N)),
        )
        down = remote(
            res.at[rnd, pl.ds(8, 8)], to, hal_s.at[rnd, 1], hal_r.at[x, layer],
            (at_layer, lax.rem(group * N + N * N * N - 1, N * N * N)),
        )
        return done, up, down

    def start_share(shared):
        done, up, down = shared

        @pl.when(group < N * N - 1)
        def _():
            up.start()

        @pl.when(group > 0)
        def _():
            down.start()

        for c in done:
            c.start()

    def sent_share(shared):
        done, up, down = shared

        @pl.when(group < N * N - 1)
        def _():
            up.wait_send()

        @pl.when(group > 0)
        def _():
            down.wait_send()

        for c in done[:-2] + done[-1:]:
            c.wait_send()

    own_src.wait()
    for p in pairs:
        source_copies[p].wait_recv()
    sent = first_stage(0)
    sent += second_stage(0)
    res[0, 8 : N * rows + 8] = product(0)

    entry = xin[1, z, y].reshape(N * rows, LANES).astype(F32) + res[0, 8 : N * rows + 8].astype(F32)
    xin[1, z, y] = entry.astype(BF16).reshape(N, rows, LANES)
    sent2 = first_stage(1)
    shared = share(0)
    start_share(shared)

    own_88.wait()
    edge_up = remote(
        src.at[0, pl.ds(rows - 8, 8)], own88.at[pl.ds(0, 8)], edge_s.at[0], edge_r.at[0],
        (layer, lax.rem(row + 1, N * N * N)),
    )
    edge_down = remote(
        src.at[0, pl.ds(0, 8)], own88.at[pl.ds(rows + 8, 8)], edge_s.at[1], edge_r.at[1],
        (layer, lax.rem(row + N * N * N - 1, N * N * N)),
    )
    last = N * N * N - 1

    @pl.when(row < last)
    def _():
        edge_up.start()

    @pl.when(row > 0)
    def _():
        edge_down.start()

    sent2 += second_stage(1)
    for c in sent:
        c.wait_send()
    for p in pairs:
        source_copies[p].wait_send()
    other_copy.wait()

    @pl.when(row < last)
    def _():
        edge_up.wait_send()
        edge_down.wait_recv()

    @pl.when(row > 0)
    def _():
        edge_down.wait_send()
        edge_up.wait_recv()

    sent_share(shared)
    res[1, 8 : N * rows + 8] = product(1)
    shared2 = share(1)
    start_share(shared2)
    for c in sent2:
        c.wait_send()
    for dx in (1, 2, 3):
        for c in range(N):
            green_copy(dx, c, gd, 0).wait_send()
    for dx in range(N):
        for c in range(N):
            forward(dx, c).wait_send()

    sent_share(shared2)

    for done, _, _ in (shared, shared2):
        done[-2].wait()
        for c in done[:-2] + done[-1:]:
            c.wait_recv()

    def wait_halo():
        for a in range(N):
            for b in range(2):
                remote(
                    res.at[0, pl.ds(0, 8)], hal.at[0, 0], hal_s.at[0, 0], hal_r.at[a, b],
                    device(sib, z, y, x),
                ).wait_recv()

    for q in range(4):
        cols = slice(q * LANES, (q + 1) * LANES)
        wave[:, cols] = (
            own88[:, cols].astype(F32) + fin[0, layer, q].astype(F32) + fin[1, layer, q].astype(F32)
        )

    def edge(at):
        wait_halo()
        for q in range(4):
            cols = slice(q * LANES, (q + 1) * LANES)
            wave[at : at + 8, cols] = (
                own88[at : at + 8, cols].astype(F32) + hal[0, q].astype(F32) + hal[1, q].astype(F32)
            )

    @pl.when(jnp.logical_and(x == 0, group > 0))
    def _():
        edge(0)

    @pl.when(jnp.logical_and(x == N - 1, group < N * N - 1))
    def _():
        edge(rows + 8)

    @pl.when(row == 0)
    def _():
        wave[0:8] = jnp.zeros((8, wave.shape[1]), F32)

    @pl.when(row == last)
    def _():
        wave[rows + 8 :] = jnp.zeros((8, wave.shape[1]), F32)

    here = layer.astype(F32)
    for q in range(4):
        cols = slice(q * LANES, (q + 1) * LANES)
        a = wave[8 : rows + 8, cols]
        b = wave[7 : rows + 7, cols] + wave[9 : rows + 9, cols]
        o = (
            other[:, cols].astype(F32)
            + fin[0, sib, q, 8 : rows + 8].astype(F32)
            + fin[1, sib, q, 8 : rows + 8].astype(F32)
        )
        for k in range(4):
            value = kc[k] * a - kf[k] * b
            if k == 0:
                value = value - kf[k] * (o * (0.25 * here))
            if k == 3:
                value = value - kf[k] * (o * (4.0 * (1.0 - here)))
            out[k, :, cols] = value.astype(BF16)


def local(source, green_down, green_up, material, pml_cells):
    rows, columns = source.shape[1:]
    points = green_down.shape[2]
    dma = pltpu.SemaphoreType.DMA
    hbm, vmem = pl.BlockSpec(memory_space=pl.ANY), pl.BlockSpec(memory_space=pltpu.VMEM)
    return pl.pallas_call(
        kernel,
        out_shape=jax.ShapeDtypeStruct((4, rows, columns), BF16),
        in_specs=[hbm, hbm, hbm, vmem, pl.BlockSpec(memory_space=pltpu.SMEM)],
        out_specs=vmem,
        scratch_shapes=[
            pltpu.VMEM((2, N, N, rows, points // N), BF16),
            pltpu.VMEM((2, N, N, N, rows, LANES), BF16),
            pltpu.VMEM((2, N * rows + 16, LANES), BF16),
            pltpu.VMEM((2, 2, 4, rows + 16, LANES), BF16),
            pltpu.VMEM((2, 4, 8, LANES), BF16),
            pltpu.VMEM((rows + 16, columns), BF16),
            pltpu.VMEM((rows, columns), BF16),
            pltpu.VMEM((rows + 16, columns), F32),
            pltpu.VMEM((4, rows, LANES), F32),
            pltpu.VMEM((4, rows, LANES), F32),
            pltpu.VMEM((8, LANES), F32),
            dma((N, N)), dma((N, N)), dma((N, N)), dma((N, N)),
            dma((2, N)), dma((2, N)),
            dma((2, 2, N, N)), dma((2, 2, N, N)),
            dma((2, 2, N)), dma((2, 2, N)),
            dma((2, 2)), dma((N, 2)),
            dma((3,)), dma((3,)),
            dma((8,)),
        ],
        compiler_params=pltpu.CompilerParams(
            collective_id=0, has_side_effects=True, vmem_limit_bytes=48 << 20
        ),
    )(source, green_down, green_up, material, pml_cells)


def solution(mesh):
    return jax.shard_map(
        local,
        mesh=mesh,
        in_specs=(
            P("layer", "row", None),
            P("layer", "row", None),
            P("layer", "row", None),
            P("layer", "row"),
            P(),
        ),
        out_specs=P("layer", "row", None),
        check_vma=False,
    )
```

```python
import functools

import jax
import jax.numpy as jnp
from jax import lax
from jax.experimental import pallas as pl
from jax.experimental.pallas import tpu as pltpu
from jax.sharding import PartitionSpec as P

MESH = pl.DeviceIdType.MESH
F32, BF16 = jnp.float32, jnp.bfloat16
N = 4
LANES = 128


def device(layer, z, y, x):
    return (layer, (z * N + y) * N + x)


def kernel(
    src, gd, gu, mat, pml, out,
    green, xin, res, fin, hal, own88, other, wave, kc, kf, mt,
    bulk_s, bulk_r, fwd_s, fwd_r, src_s, src_r, x_s, x_r, fin_s, fin_r,
    hal_s, hal_r, edge_s, edge_r, loc,
):
    layer = lax.axis_index("layer")
    row = lax.axis_index("row")
    z, y, x = row // (N * N), (row // N) % N, row % N
    group = z * N + y
    rows = src.shape[1]
    chunk = N * N * rows
    sweep = x // 2
    sib = 1 - layer
    mine = (layer + sweep) % 2

    def shift(a, d):
        return lax.rem(a + d, N)

    def remote(s, d, ss, rs, to):
        return pltpu.make_async_remote_copy(
            src_ref=s, dst_ref=d, send_sem=ss, recv_sem=rs, device_id=to, device_id_type=MESH
        )

    greet = [device(sib, z, y, x)]
    for d in (1, 2, 3):
        greet += [device(layer, z, y, shift(x, d)), device(sib, z, y, shift(x, d))]
        greet += [device(layer, z, shift(y, d), x), device(layer, shift(z, d), y, x)]
    barrier = pltpu.get_barrier_semaphore()
    for to in greet:
        pl.semaphore_signal(barrier, inc=1, device_id=to, device_id_type=MESH)

    def green_part(ref, c):
        return ref.at[0, :, pl.ds(pl.multiple_of(shift(z, c) * chunk, LANES), chunk)]

    def part_of_source(to_x, to_layer):
        quarter = 2 * lax.rem(to_x, 2) + to_layer
        return src.at[0, :, pl.ds(pl.multiple_of(quarter * LANES, LANES), LANES)]

    own_src = pltpu.make_async_copy(part_of_source(x, layer), xin.at[mine, z, y, x], loc.at[0])
    own_src.start()
    own_88 = pltpu.make_async_copy(src.at[0], own88.at[pl.ds(8, rows)], loc.at[1])
    own_88.start()
    own_green = []
    for c in range(N):
        to = green.at[mine, shift(z, c), x]
        for s, ref in ((0, gd), (1, gu)):
            @pl.when(sweep == s)
            def _(ref=ref, to=to, c=c):
                pltpu.make_async_copy(green_part(ref, c), to, loc.at[2 + c]).start()
        own_green.append(pltpu.make_async_copy(green_part(gd, c), to, loc.at[2 + c]))

    pl.semaphore_wait(barrier, len(greet))

    def source_copy(dx, dl):
        to_x = shift(x, dx)
        to_l = layer if dl == 0 else sib
        rnd = (layer + to_x // 2) % 2
        return remote(
            part_of_source(to_x, to_l), xin.at[rnd, z, y, x], src_s.at[dl, dx], src_r.at[dl, dx],
            device(to_l, z, y, to_x),
        )

    pairs = [(dx, dl) for dx in (2, 1, 3, 0) for dl in (0, 1) if (dx, dl) != (0, 0)]
    source_copies = {p: source_copy(*p) for p in pairs}
    for p in pairs:
        source_copies[p].start()

    mate = x + 1 - 2 * (x % 2)
    outer = lax.rem(x + N - 1 + 2 * (x % 2), N)
    far = shift(x, 2)
    OWN, MATE, OUTER, FAR = range(4)
    place = {OWN: x, MATE: mate, OUTER: outer, FAR: far}
    order = (0, 1, 3, 2)

    def to_mate(c, ref):
        return remote(
            green_part(ref, c), green.at[mine, shift(z, c), x],
            bulk_s.at[MATE, c], bulk_r.at[MATE, c], device(layer, z, y, mate),
        )

    def to_outer(c, ref):
        return remote(
            green_part(ref, c), green.at[1 - mine, shift(z, c), x],
            bulk_s.at[OUTER, c], bulk_r.at[OUTER, c], device(layer, z, y, outer),
        )

    def far_to_mate(c):
        at = green.at[mine, shift(z, c), outer]
        return remote(at, at, bulk_s.at[FAR, c], bulk_r.at[FAR, c], device(layer, z, y, mate))

    def to_sibling(kind, c, ref=None):
        at = green.at[mine, shift(z, c), place[kind]]
        return remote(
            at if ref is None else green_part(ref, c), at, fwd_s.at[kind, c], fwd_r.at[kind, c],
            device(sib, z, y, x),
        )

    def send_own(refs, other):
        for s, ref in ((0, refs[0]), (1, refs[1])):
            @pl.when(sweep == s)
            def _(ref=ref):
                for c in order:
                    (to_outer if other else to_mate)(c, ref).start()

    def own_to_sibling():
        for s, ref in ((0, gd), (1, gu)):
            @pl.when(sweep == s)
            def _(ref=ref):
                for c in order:
                    to_sibling(OWN, c, ref).start()

    def relay(c):
        to_outer(c, gd).wait_recv()
        far_to_mate(c).start()
        to_sibling(OUTER, c).start()

    @pl.when(mine == 0)
    def _():
        send_own((gd, gu), False)

    @pl.when(mine == 1)
    def _():
        send_own((gu, gd), True)

    own_to_sibling()

    other_copy = remote(src.at[0], other, edge_s.at[2], edge_r.at[2], device(sib, z, y, x))
    other_copy.start()

    rows_at = lax.broadcasted_iota(jnp.int32, (rows, LANES), 0) + row * rows
    thick = jnp.full((rows, LANES), pml[0].astype(F32))
    total = rows * N * N * N

    def ramp(index, count):
        dist = jnp.minimum(index, count - 1 - index).astype(F32)
        return jnp.maximum(thick - dist, 0.0) / thick

    ramp_m = ramp(rows_at, total)
    mt[...] = jnp.zeros_like(mt)
    mt[0:4, 0:rows] = 1.0 + 1.5 * mat[...].astype(F32)
    kappa = mt[...].T
    for k in range(4):
        ramp_z = ramp(jnp.full((rows, LANES), layer * 4 + k, jnp.int32), 8)
        sigma = 3.0 * (ramp_z * ramp_z + ramp_m * ramp_m)
        f = (4 - k) / 4
        around = (0 if k == 0 else (5 - k) / 4) + (0 if k == 3 else (3 - k) / 4)
        kap = jnp.broadcast_to(kappa[0:rows, k : k + 1], (rows, LANES))
        kc[k] = kap * (f * (4.0 + sigma) - around)
        kf[k] = kap * f
    res[:, 0:8] = jnp.zeros((2, 8, LANES), BF16)
    res[:, 4 * rows + 8 :] = jnp.zeros((2, 8, LANES), BF16)

    halves = (pl.ds(0, 2), pl.ds(2, 2))

    def plane_copy(rnd, part, from_z, from_y, sz, sy, to_z, to_y):
        at = xin.at[rnd, from_z, from_y, halves[part]]
        return remote(
            at, at, x_s.at[rnd, part, sz, sy], x_r.at[rnd, part, sz, sy],
            device(layer, to_z, to_y, x),
        )

    def first_stage(rnd):
        done = []
        for d in (2, 1, 3):
            done.append(plane_copy(rnd, 0, z, y, 0, d, z, shift(y, d)))
            done.append(plane_copy(rnd, 1, z, y, d, 0, shift(z, d), y))
        for d in (2, 1, 3):
            done.append(plane_copy(rnd, 0, z, y, d, 0, shift(z, d), y))
            done.append(plane_copy(rnd, 1, z, y, 0, d, z, shift(y, d)))
        for c in done:
            c.start()
        return done

    def arrival(rnd, part, sz, sy):
        from_z, from_y = shift(z, N - sz), shift(y, N - sy)
        at = xin.at[rnd, from_z, from_y, halves[part]]
        return remote(
            at, at, x_s.at[rnd, part, sz, sy], x_r.at[rnd, part, sz, sy], device(layer, z, y, x)
        )

    def second_stage(rnd):
        done = []
        for d in (1, 3, 2):
            if rnd == 0:
                @pl.when(mine == 0)
                def _(d=d):
                    relay(order[(0, 0, 2, 1)[d]])
            arrival(rnd, 0, 0, d).wait_recv()
            for q in (2, 1, 3):
                done.append(plane_copy(rnd, 0, z, shift(y, N - d), q, d, shift(z, q), y))
                done[-1].start()
            arrival(rnd, 1, d, 0).wait_recv()
            for q in (2, 1, 3):
                done.append(plane_copy(rnd, 1, shift(z, N - d), y, d, q, z, shift(y, q)))
                done[-1].start()
        return done

    def wait_plane(rnd, sz):
        for sy in (0, 1, 3, 2):
            for part in (0, 1):
                if (sz, sy) != (0, 0) and not (part == 0 and sz == 0) and not (part == 1 and sy == 0):
                    arrival(rnd, part, sz, sy).wait_recv()

    def wait_green(rnd, c):
        @pl.when(mine == rnd)
        def _():
            to_mate(c, gd).wait_recv()
            to_sibling(MATE, c).start()
            far_to_mate(c).wait_recv()
            to_sibling(FAR, c).start()
            own_green[c].wait()

        @pl.when(mine != rnd)
        def _():
            for kind in (OWN, OUTER, MATE, FAR):
                to_sibling(kind, c).wait_recv()

    def product(rnd):
        acc = None
        for c in order:
            wait_green(rnd, c)
            wait_plane(rnd, (N - c) % N)
            g = green[rnd, shift(z, c)].reshape(N * rows, chunk)
            v = xin[rnd, shift(z, c)].reshape(chunk, LANES)
            term = jnp.dot(g, v, preferred_element_type=F32)
            acc = term if acc is None else acc + term
        return acc.astype(BF16)

    def share(rnd):
        at_layer = sweep if rnd == 0 else 1 - sweep
        quarter = 2 * lax.rem(x, 2) + layer
        done = []
        for dx in (2, 1, 3, 0):
            to_x = shift(x, dx)
            at = res.at[rnd, pl.ds(pl.multiple_of(to_x * rows, 8), rows + 16)]
            to = fin.at[sweep, at_layer, quarter]
            for dl in (0, 1):
                if (dx, dl) == (0, 0):
                    done.append(pltpu.make_async_copy(at, to, loc.at[6 + rnd]))
                else:
                    done.append(remote(
                        at, to, fin_s.at[rnd, dl, dx], fin_r.at[rnd, dl, dx],
                        device(layer if dl == 0 else sib, z, y, to_x),
                    ))
        to = hal.at[sweep, quarter]
        up = remote(
            res.at[rnd, pl.ds(N * rows, 8)], to, hal_s.at[rnd, 0], hal_r.at[x, layer],
            (at_layer, lax.rem((group + 1) * N, N * N * N)),
        )
        down = remote(
            res.at[rnd, pl.ds(8, 8)], to, hal_s.at[rnd, 1], hal_r.at[x, layer],
            (at_layer, lax.rem(group * N + N * N * N - 1, N * N * N)),
        )
        return done, up, down

    def start_share(shared):
        done, up, down = shared

        @pl.when(group < N * N - 1)
        def _():
            up.start()

        @pl.when(group > 0)
        def _():
            down.start()

        for c in done:
            c.start()

    def sent_share(shared):
        done, up, down = shared

        @pl.when(group < N * N - 1)
        def _():
            up.wait_send()

        @pl.when(group > 0)
        def _():
            down.wait_send()

        for c in done[:-2] + done[-1:]:
            c.wait_send()

    own_src.wait()
    for p in pairs:
        source_copies[p].wait_recv()
    sent = first_stage(0)
    sent += second_stage(0)

    @pl.when(mine == 0)
    def _():
        relay(order[3])
        send_own((gu, gd), True)

    @pl.when(mine == 1)
    def _():
        send_own((gd, gu), False)

    res[0, 8 : N * rows + 8] = product(0)

    entry = xin[1, z, y].reshape(N * rows, LANES).astype(F32) + res[0, 8 : N * rows + 8].astype(F32)
    xin[1, z, y] = entry.astype(BF16).reshape(N, rows, LANES)
    sent2 = first_stage(1)
    shared = share(0)
    start_share(shared)

    own_88.wait()
    edge_up = remote(
        src.at[0, pl.ds(rows - 8, 8)], own88.at[pl.ds(0, 8)], edge_s.at[0], edge_r.at[0],
        (layer, lax.rem(row + 1, N * N * N)),
    )
    edge_down = remote(
        src.at[0, pl.ds(0, 8)], own88.at[pl.ds(rows + 8, 8)], edge_s.at[1], edge_r.at[1],
        (layer, lax.rem(row + N * N * N - 1, N * N * N)),
    )
    last = N * N * N - 1

    @pl.when(row < last)
    def _():
        edge_up.start()

    @pl.when(row > 0)
    def _():
        edge_down.start()


    @pl.when(mine == 1)
    def _():
        for c in order:
            relay(c)

    sent2 += second_stage(1)
    res[1, 8 : N * rows + 8] = product(1)
    shared2 = share(1)
    start_share(shared2)

    for c in sent + sent2:
        c.wait_send()
    for p in pairs:
        source_copies[p].wait_send()
    other_copy.wait()

    @pl.when(row < last)
    def _():
        edge_up.wait_send()
        edge_down.wait_recv()

    @pl.when(row > 0)
    def _():
        edge_down.wait_send()
        edge_up.wait_recv()

    sent_share(shared)
    for c in range(N):
        to_mate(c, gd).wait_send()
        to_outer(c, gd).wait_send()
        far_to_mate(c).wait_send()
        for kind in range(4):
            to_sibling(kind, c).wait_send()
    sent_share(shared2)

    for done, _, _ in (shared, shared2):
        done[-2].wait()
        for c in done[:-2] + done[-1:]:
            c.wait_recv()

    def wait_halo():
        for a in range(N):
            for b in range(2):
                remote(
                    res.at[0, pl.ds(0, 8)], hal.at[0, 0], hal_s.at[0, 0], hal_r.at[a, b],
                    device(sib, z, y, x),
                ).wait_recv()

    for q in range(4):
        cols = slice(q * LANES, (q + 1) * LANES)
        wave[:, cols] = (
            own88[:, cols].astype(F32) + fin[0, layer, q].astype(F32) + fin[1, layer, q].astype(F32)
        )

    def edge(at):
        wait_halo()
        for q in range(4):
            cols = slice(q * LANES, (q + 1) * LANES)
            wave[at : at + 8, cols] = (
                own88[at : at + 8, cols].astype(F32) + hal[0, q].astype(F32) + hal[1, q].astype(F32)
            )

    @pl.when(jnp.logical_and(x == 0, group > 0))
    def _():
        edge(0)

    @pl.when(jnp.logical_and(x == N - 1, group < N * N - 1))
    def _():
        edge(rows + 8)

    @pl.when(row == 0)
    def _():
        wave[0:8] = jnp.zeros((8, wave.shape[1]), F32)

    @pl.when(row == last)
    def _():
        wave[rows + 8 :] = jnp.zeros((8, wave.shape[1]), F32)

    here = layer.astype(F32)
    for q in range(4):
        cols = slice(q * LANES, (q + 1) * LANES)
        a = wave[8 : rows + 8, cols]
        b = wave[7 : rows + 7, cols] + wave[9 : rows + 9, cols]
        o = (
            other[:, cols].astype(F32)
            + fin[0, sib, q, 8 : rows + 8].astype(F32)
            + fin[1, sib, q, 8 : rows + 8].astype(F32)
        )
        for k in range(4):
            value = kc[k] * a - kf[k] * b
            if k == 0:
                value = value - kf[k] * (o * (0.25 * here))
            if k == 3:
                value = value - kf[k] * (o * (4.0 * (1.0 - here)))
            out[k, :, cols] = value.astype(BF16)


def local(source, green_down, green_up, material, pml_cells):
    rows, columns = source.shape[1:]
    points = green_down.shape[2]
    dma = pltpu.SemaphoreType.DMA
    hbm, vmem = pl.BlockSpec(memory_space=pltpu.HBM), pl.BlockSpec(memory_space=pltpu.VMEM)
    return pl.pallas_call(
        kernel,
        out_shape=jax.ShapeDtypeStruct((4, rows, columns), BF16),
        in_specs=[hbm, hbm, hbm, vmem, pl.BlockSpec(memory_space=pltpu.SMEM)],
        out_specs=vmem,
        scratch_shapes=[
            pltpu.VMEM((2, N, N, rows, points // N), BF16),
            pltpu.VMEM((2, N, N, N, rows, LANES), BF16),
            pltpu.VMEM((2, N * rows + 16, LANES), BF16),
            pltpu.VMEM((2, 2, 4, rows + 16, LANES), BF16),
            pltpu.VMEM((2, 4, 8, LANES), BF16),
            pltpu.VMEM((rows + 16, columns), BF16),
            pltpu.VMEM((rows, columns), BF16),
            pltpu.VMEM((rows + 16, columns), F32),
            pltpu.VMEM((4, rows, LANES), F32),
            pltpu.VMEM((4, rows, LANES), F32),
            pltpu.VMEM((8, LANES), F32),
            dma((N, N)), dma((N, N)), dma((N, N)), dma((N, N)),
            dma((2, N)), dma((2, N)),
            dma((2, 2, N, N)), dma((2, 2, N, N)),
            dma((2, 2, N)), dma((2, 2, N)),
            dma((2, 2)), dma((N, 2)),
            dma((3,)), dma((3,)),
            dma((8,)),
        ],
        compiler_params=pltpu.CompilerParams(
            collective_id=0, has_side_effects=True, vmem_limit_bytes=60 << 20
        ),
    )(source, green_down, green_up, material, pml_cells)


def solution(mesh):
    return jax.shard_map(
        local,
        mesh=mesh,
        in_specs=(
            P("layer", "row", None),
            P("layer", "row", None),
            P("layer", "row", None),
            P("layer", "row"),
            P(),
        ),
        out_specs=P("layer", "row", None),
        check_vma=False,
    )
```

```python
import functools

import jax
import jax.numpy as jnp
from jax import lax
from jax.experimental import pallas as pl
from jax.experimental.pallas import tpu as pltpu
from jax.sharding import PartitionSpec as P

MESH = pl.DeviceIdType.MESH
F32, BF16 = jnp.float32, jnp.bfloat16
N = 4
LANES = 128


def device(layer, z, y, x):
    return (layer, (z * N + y) * N + x)


def kernel(
    src, gd, gu, mat, pml, out,
    pml_s, mat_v, green, xin, res, fin, hal, own88, other, wave, kc, kf, mt,
    bulk_s, bulk_r, fwd_s, fwd_r, src_s, src_r, x_s, x_r, fin_s, fin_r,
    hal_s, hal_r, edge_s, edge_r, loc,
):
    layer = lax.axis_index("layer")
    row = lax.axis_index("row")
    z, y, x = row // (N * N), (row // N) % N, row % N
    group = z * N + y
    rows = src.shape[1]
    chunk = N * N * rows
    sweep = x // 2
    sib = 1 - layer
    mine = (layer + sweep) % 2

    def shift(a, d):
        return lax.rem(a + d, N)

    def remote(s, d, ss, rs, to):
        return pltpu.make_async_remote_copy(
            src_ref=s, dst_ref=d, send_sem=ss, recv_sem=rs, device_id=to, device_id_type=MESH
        )

    greet = [device(sib, z, y, x)]
    for d in (1, 2, 3):
        greet += [device(layer, z, y, shift(x, d)), device(sib, z, y, shift(x, d))]
        greet += [device(layer, z, shift(y, d), x), device(layer, shift(z, d), y, x)]
    barrier = pltpu.get_barrier_semaphore()
    for to in greet:
        pl.semaphore_signal(barrier, inc=1, device_id=to, device_id_type=MESH)

    def green_part(ref, c):
        return ref.at[0, :, pl.ds(pl.multiple_of(shift(z, c) * chunk, LANES), chunk)]

    own_rows = own88.at[pl.ds(8, rows)]

    def quarter_of(to_x, to_layer):
        return pl.ds(pl.multiple_of((2 * lax.rem(to_x, 2) + to_layer) * LANES, LANES), LANES)

    pml_copy = pltpu.make_async_copy(pml, pml_s, loc.at[8])
    pml_copy.start()
    mat_copy = pltpu.make_async_copy(mat, mat_v, loc.at[9])
    mat_copy.start()
    own_src = pltpu.make_async_copy(
        src.at[0, :, quarter_of(x, layer)], xin.at[mine, z, y, x], loc.at[0]
    )
    own_src.start()
    own_88 = pltpu.make_async_copy(src.at[0], own_rows, loc.at[1])
    own_88.start()
    own_green = []
    for c in range(N):
        to = green.at[mine, shift(z, c), x]
        for s, ref in ((0, gd), (1, gu)):
            @pl.when(sweep == s)
            def _(ref=ref, to=to, c=c):
                pltpu.make_async_copy(green_part(ref, c), to, loc.at[2 + c]).start()
        own_green.append(pltpu.make_async_copy(green_part(gd, c), to, loc.at[2 + c]))

    own_88.wait()
    pl.semaphore_wait(barrier, len(greet))

    def source_copy(dx, dl):
        to_x = shift(x, dx)
        to_l = layer if dl == 0 else sib
        rnd = (layer + to_x // 2) % 2
        return remote(
            own88.at[pl.ds(8, rows), quarter_of(to_x, to_l)], xin.at[rnd, z, y, x], src_s.at[dl, dx], src_r.at[dl, dx],
            device(to_l, z, y, to_x),
        )

    pairs = [(dx, dl) for dx in (2, 1, 3, 0) for dl in (0, 1) if (dx, dl) != (0, 0)]
    source_copies = {p: source_copy(*p) for p in pairs}
    for p in pairs:
        source_copies[p].start()

    mate = x + 1 - 2 * (x % 2)
    outer = lax.rem(x + N - 1 + 2 * (x % 2), N)
    far = shift(x, 2)
    OWN, MATE, OUTER, FAR = range(4)
    place = {OWN: x, MATE: mate, OUTER: outer, FAR: far}
    order = (0, 1, 3, 2)

    def to_mate(c, ref):
        return remote(
            green_part(ref, c), green.at[mine, shift(z, c), x],
            bulk_s.at[MATE, c], bulk_r.at[MATE, c], device(layer, z, y, mate),
        )

    def to_outer(c, ref):
        return remote(
            green_part(ref, c), green.at[1 - mine, shift(z, c), x],
            bulk_s.at[OUTER, c], bulk_r.at[OUTER, c], device(layer, z, y, outer),
        )

    def far_to_mate(c):
        at = green.at[mine, shift(z, c), outer]
        return remote(at, at, bulk_s.at[FAR, c], bulk_r.at[FAR, c], device(layer, z, y, mate))

    def to_sibling(kind, c, ref=None):
        at = green.at[mine, shift(z, c), place[kind]]
        return remote(
            at if ref is None else green_part(ref, c), at, fwd_s.at[kind, c], fwd_r.at[kind, c],
            device(sib, z, y, x),
        )

    def send_own(refs, other):
        for s, ref in ((0, refs[0]), (1, refs[1])):
            @pl.when(sweep == s)
            def _(ref=ref):
                for c in order:
                    (to_outer if other else to_mate)(c, ref).start()

    def own_to_sibling():
        for s, ref in ((0, gd), (1, gu)):
            @pl.when(sweep == s)
            def _(ref=ref):
                for c in order:
                    to_sibling(OWN, c, ref).start()

    def relay(c):
        to_outer(c, gd).wait_recv()
        far_to_mate(c).start()
        to_sibling(OUTER, c).start()

    @pl.when(mine == 0)
    def _():
        send_own((gd, gu), False)

    @pl.when(mine == 1)
    def _():
        send_own((gu, gd), True)

    own_to_sibling()

    other_copy = remote(own_rows, other, edge_s.at[2], edge_r.at[2], device(sib, z, y, x))
    other_copy.start()

    pml_copy.wait()
    mat_copy.wait()
    rows_at = lax.broadcasted_iota(jnp.int32, (rows, LANES), 0) + row * rows
    thick = jnp.full((rows, LANES), pml_s[0].astype(F32))
    total = rows * N * N * N

    def ramp(index, count):
        dist = jnp.minimum(index, count - 1 - index).astype(F32)
        return jnp.maximum(thick - dist, 0.0) / thick

    ramp_m = ramp(rows_at, total)
    mt[...] = jnp.zeros_like(mt)
    mt[0:4, 0:rows] = 1.0 + 1.5 * mat_v[...].astype(F32)
    kappa = mt[...].T
    for k in range(4):
        ramp_z = ramp(jnp.full((rows, LANES), layer * 4 + k, jnp.int32), 8)
        sigma = 3.0 * (ramp_z * ramp_z + ramp_m * ramp_m)
        f = (4 - k) / 4
        around = (0 if k == 0 else (5 - k) / 4) + (0 if k == 3 else (3 - k) / 4)
        kap = jnp.broadcast_to(kappa[0:rows, k : k + 1], (rows, LANES))
        kc[k] = kap * (f * (4.0 + sigma) - around)
        kf[k] = kap * f
    res[:, 0:8] = jnp.zeros((2, 8, LANES), BF16)
    res[:, 4 * rows + 8 :] = jnp.zeros((2, 8, LANES), BF16)

    halves = (pl.ds(0, 2), pl.ds(2, 2))

    def plane_copy(rnd, part, from_z, from_y, sz, sy, to_z, to_y):
        at = xin.at[rnd, from_z, from_y, halves[part]]
        return remote(
            at, at, x_s.at[rnd, part, sz, sy], x_r.at[rnd, part, sz, sy],
            device(layer, to_z, to_y, x),
        )

    def first_stage(rnd):
        done = []
        for d in (2, 1, 3):
            done.append(plane_copy(rnd, 0, z, y, 0, d, z, shift(y, d)))
            done.append(plane_copy(rnd, 1, z, y, d, 0, shift(z, d), y))
        for d in (2, 1, 3):
            done.append(plane_copy(rnd, 0, z, y, d, 0, shift(z, d), y))
            done.append(plane_copy(rnd, 1, z, y, 0, d, z, shift(y, d)))
        for c in done:
            c.start()
        return done

    def arrival(rnd, part, sz, sy):
        from_z, from_y = shift(z, N - sz), shift(y, N - sy)
        at = xin.at[rnd, from_z, from_y, halves[part]]
        return remote(
            at, at, x_s.at[rnd, part, sz, sy], x_r.at[rnd, part, sz, sy], device(layer, z, y, x)
        )

    def second_stage(rnd):
        done = []
        for d in (1, 3, 2):
            if rnd == 0:
                @pl.when(mine == 0)
                def _(d=d):
                    relay(order[(0, 0, 2, 1)[d]])
            arrival(rnd, 0, 0, d).wait_recv()
            for q in (2, 1, 3):
                done.append(plane_copy(rnd, 0, z, shift(y, N - d), q, d, shift(z, q), y))
                done[-1].start()
            arrival(rnd, 1, d, 0).wait_recv()
            for q in (2, 1, 3):
                done.append(plane_copy(rnd, 1, shift(z, N - d), y, d, q, z, shift(y, q)))
                done[-1].start()
        return done

    def wait_plane(rnd, sz):
        for sy in (0, 1, 3, 2):
            for part in (0, 1):
                if (sz, sy) != (0, 0) and not (part == 0 and sz == 0) and not (part == 1 and sy == 0):
                    arrival(rnd, part, sz, sy).wait_recv()

    def wait_green(rnd, c):
        @pl.when(mine == rnd)
        def _():
            to_mate(c, gd).wait_recv()
            to_sibling(MATE, c).start()
            far_to_mate(c).wait_recv()
            to_sibling(FAR, c).start()
            own_green[c].wait()

        @pl.when(mine != rnd)
        def _():
            for kind in (OWN, OUTER, MATE, FAR):
                to_sibling(kind, c).wait_recv()

    def product(rnd):
        acc = None
        for c in order:
            wait_green(rnd, c)
            if rnd == 0 and c == order[1]:
                @pl.when(mine == 1)
                def _():
                    send_own((gd, gu), False)
            wait_plane(rnd, (N - c) % N)
            g = green[rnd, shift(z, c)].reshape(N * rows, chunk)
            v = xin[rnd, shift(z, c)].reshape(chunk, LANES)
            term = jnp.dot(g, v, preferred_element_type=F32)
            acc = term if acc is None else acc + term
        return acc.astype(BF16)

    def share(rnd):
        at_layer = sweep if rnd == 0 else 1 - sweep
        quarter = 2 * lax.rem(x, 2) + layer
        done = []
        for dx in (2, 1, 3, 0):
            to_x = shift(x, dx)
            at = res.at[rnd, pl.ds(pl.multiple_of(to_x * rows, 8), rows + 16)]
            to = fin.at[sweep, at_layer, quarter]
            for dl in (0, 1):
                if (dx, dl) == (0, 0):
                    done.append(pltpu.make_async_copy(at, to, loc.at[6 + rnd]))
                else:
                    done.append(remote(
                        at, to, fin_s.at[rnd, dl, dx], fin_r.at[rnd, dl, dx],
                        device(layer if dl == 0 else sib, z, y, to_x),
                    ))
        to = hal.at[sweep, quarter]
        up = remote(
            res.at[rnd, pl.ds(N * rows, 8)], to, hal_s.at[rnd, 0], hal_r.at[x, layer],
            (at_layer, lax.rem((group + 1) * N, N * N * N)),
        )
        down = remote(
            res.at[rnd, pl.ds(8, 8)], to, hal_s.at[rnd, 1], hal_r.at[x, layer],
            (at_layer, lax.rem(group * N + N * N * N - 1, N * N * N)),
        )
        return done, up, down

    def start_share(shared):
        done, up, down = shared

        @pl.when(group < N * N - 1)
        def _():
            up.start()

        @pl.when(group > 0)
        def _():
            down.start()

        for c in done:
            c.start()

    def sent_share(shared):
        done, up, down = shared

        @pl.when(group < N * N - 1)
        def _():
            up.wait_send()

        @pl.when(group > 0)
        def _():
            down.wait_send()

        for c in done[:-2] + done[-1:]:
            c.wait_send()

    def wait_sources(same_core):
        if same_core:
            own_src.wait()
        for p in pairs:
            if p[1] == (0 if same_core else 1):
                source_copies[p].wait_recv()

    for m in (0, 1):
        @pl.when(mine == m)
        def _(m=m):
            wait_sources(m == 0)
    sent = first_stage(0)
    sent += second_stage(0)

    @pl.when(mine == 0)
    def _():
        relay(order[3])
        send_own((gu, gd), True)

    res[0, 8 : N * rows + 8] = product(0)

    for m in (0, 1):
        @pl.when(mine == m)
        def _(m=m):
            wait_sources(m == 1)
    entry = xin[1, z, y].reshape(N * rows, LANES).astype(F32) + res[0, 8 : N * rows + 8].astype(F32)
    xin[1, z, y] = entry.astype(BF16).reshape(N, rows, LANES)
    sent2 = first_stage(1)
    shared = share(0)
    start_share(shared)

    edge_up = remote(
        own88.at[pl.ds(rows, 8)], own88.at[pl.ds(0, 8)], edge_s.at[0], edge_r.at[0],
        (layer, lax.rem(row + 1, N * N * N)),
    )
    edge_down = remote(
        own88.at[pl.ds(8, 8)], own88.at[pl.ds(rows + 8, 8)], edge_s.at[1], edge_r.at[1],
        (layer, lax.rem(row + N * N * N - 1, N * N * N)),
    )
    last = N * N * N - 1

    @pl.when(row < last)
    def _():
        edge_up.start()

    @pl.when(row > 0)
    def _():
        edge_down.start()


    @pl.when(mine == 1)
    def _():
        for c in order:
            relay(c)

    sent2 += second_stage(1)
    res[1, 8 : N * rows + 8] = product(1)
    shared2 = share(1)
    start_share(shared2)

    for c in sent + sent2:
        c.wait_send()
    for p in pairs:
        source_copies[p].wait_send()
    other_copy.wait()

    @pl.when(row < last)
    def _():
        edge_up.wait_send()
        edge_down.wait_recv()

    @pl.when(row > 0)
    def _():
        edge_down.wait_send()
        edge_up.wait_recv()

    sent_share(shared)
    for c in range(N):
        to_mate(c, gd).wait_send()
        to_outer(c, gd).wait_send()
        far_to_mate(c).wait_send()
        for kind in range(4):
            to_sibling(kind, c).wait_send()
    sent_share(shared2)

    for done, _, _ in (shared, shared2):
        done[-2].wait()
        for c in done[:-2] + done[-1:]:
            c.wait_recv()

    def wait_halo():
        for a in range(N):
            for b in range(2):
                remote(
                    res.at[0, pl.ds(0, 8)], hal.at[0, 0], hal_s.at[0, 0], hal_r.at[a, b],
                    device(sib, z, y, x),
                ).wait_recv()

    for q in range(4):
        cols = slice(q * LANES, (q + 1) * LANES)
        wave[:, cols] = (
            own88[:, cols].astype(F32) + fin[0, layer, q].astype(F32) + fin[1, layer, q].astype(F32)
        )

    def edge(at):
        wait_halo()
        for q in range(4):
            cols = slice(q * LANES, (q + 1) * LANES)
            wave[at : at + 8, cols] = (
                own88[at : at + 8, cols].astype(F32) + hal[0, q].astype(F32) + hal[1, q].astype(F32)
            )

    @pl.when(jnp.logical_and(x == 0, group > 0))
    def _():
        edge(0)

    @pl.when(jnp.logical_and(x == N - 1, group < N * N - 1))
    def _():
        edge(rows + 8)

    @pl.when(row == 0)
    def _():
        wave[0:8] = jnp.zeros((8, wave.shape[1]), F32)

    @pl.when(row == last)
    def _():
        wave[rows + 8 :] = jnp.zeros((8, wave.shape[1]), F32)

    here = layer.astype(F32)
    for q in range(4):
        cols = slice(q * LANES, (q + 1) * LANES)
        a = wave[8 : rows + 8, cols]
        b = wave[7 : rows + 7, cols] + wave[9 : rows + 9, cols]
        o = (
            other[:, cols].astype(F32)
            + fin[0, sib, q, 8 : rows + 8].astype(F32)
            + fin[1, sib, q, 8 : rows + 8].astype(F32)
        )
        for k in range(4):
            value = kc[k] * a - kf[k] * b
            if k == 0:
                value = value - kf[k] * (o * (0.25 * here))
            if k == 3:
                value = value - kf[k] * (o * (4.0 * (1.0 - here)))
            out[k, :, cols] = value.astype(BF16)


def local(source, green_down, green_up, material, pml_cells):
    rows, columns = source.shape[1:]
    points = green_down.shape[2]
    dma = pltpu.SemaphoreType.DMA
    hbm, vmem = pl.BlockSpec(memory_space=pltpu.HBM), pl.BlockSpec(memory_space=pltpu.VMEM)
    return pl.pallas_call(
        kernel,
        out_shape=jax.ShapeDtypeStruct((4, rows, columns), BF16),
        in_specs=[hbm] * 5,
        out_specs=vmem,
        scratch_shapes=[
            pltpu.SMEM((1,), jnp.int32),
            pltpu.VMEM((4, rows), jnp.int32),
            pltpu.VMEM((2, N, N, rows, points // N), BF16),
            pltpu.VMEM((2, N, N, N, rows, LANES), BF16),
            pltpu.VMEM((2, N * rows + 16, LANES), BF16),
            pltpu.VMEM((2, 2, 4, rows + 16, LANES), BF16),
            pltpu.VMEM((2, 4, 8, LANES), BF16),
            pltpu.VMEM((rows + 16, columns), BF16),
            pltpu.VMEM((rows, columns), BF16),
            pltpu.VMEM((rows + 16, columns), F32),
            pltpu.VMEM((4, rows, LANES), F32),
            pltpu.VMEM((4, rows, LANES), F32),
            pltpu.VMEM((8, LANES), F32),
            dma((N, N)), dma((N, N)), dma((N, N)), dma((N, N)),
            dma((2, N)), dma((2, N)),
            dma((2, 2, N, N)), dma((2, 2, N, N)),
            dma((2, 2, N)), dma((2, 2, N)),
            dma((2, 2)), dma((N, 2)),
            dma((3,)), dma((3,)),
            dma((10,)),
        ],
        compiler_params=pltpu.CompilerParams(
            collective_id=0, has_side_effects=True, vmem_limit_bytes=60 << 20
        ),
    )(source, green_down, green_up, material, pml_cells)


def solution(mesh):
    return jax.shard_map(
        local,
        mesh=mesh,
        in_specs=(
            P("layer", "row", None),
            P("layer", "row", None),
            P("layer", "row", None),
            P("layer", "row"),
            P(),
        ),
        out_specs=P("layer", "row", None),
        check_vma=False,
    )
```

```python
import functools

import jax
import jax.numpy as jnp
from jax import lax
from jax.experimental import pallas as pl
from jax.experimental.pallas import tpu as pltpu
from jax.sharding import PartitionSpec as P

MESH = pl.DeviceIdType.MESH
F32, BF16 = jnp.float32, jnp.bfloat16
N = 4
LANES = 128


def device(layer, z, y, x):
    return (layer, (z * N + y) * N + x)


def kernel(
    src, gd, gu, mat, pml, out,
    pml_s, mat_v, green, xin, res, fin, hal, own88, other, wave, kc, kf, mt,
    bulk_s, bulk_r, fwd_s, fwd_r, src_s, src_r, x_s, x_r, fin_s, fin_r,
    hal_s, hal_r, edge_s, edge_r, loc,
):
    layer = lax.axis_index("layer")
    row = lax.axis_index("row")
    z, y, x = row // (N * N), (row // N) % N, row % N
    group = z * N + y
    rows = src.shape[1]
    chunk = N * N * rows
    sweep = x // 2
    sib = 1 - layer
    mine = (layer + sweep) % 2

    def shift(a, d):
        return lax.rem(a + d, N)

    def remote(s, d, ss, rs, to):
        return pltpu.make_async_remote_copy(
            src_ref=s, dst_ref=d, send_sem=ss, recv_sem=rs, device_id=to, device_id_type=MESH
        )

    greet = [device(sib, z, y, x)]
    for d in (1, 2, 3):
        greet += [device(layer, z, y, shift(x, d)), device(sib, z, y, shift(x, d))]
        greet += [device(layer, z, shift(y, d), x), device(layer, shift(z, d), y, x)]
    barrier = pltpu.get_barrier_semaphore()
    for to in greet:
        pl.semaphore_signal(barrier, inc=1, device_id=to, device_id_type=MESH)

    def green_part(ref, c):
        return ref.at[0, :, pl.ds(pl.multiple_of(shift(z, c) * chunk, LANES), chunk)]

    own_rows = own88.at[pl.ds(8, rows)]

    def quarter_of(to_x, to_layer):
        return pl.ds(pl.multiple_of((2 * lax.rem(to_x, 2) + to_layer) * LANES, LANES), LANES)

    pml_copy = pltpu.make_async_copy(pml, pml_s, loc.at[8])
    pml_copy.start()
    mat_copy = pltpu.make_async_copy(mat, mat_v, loc.at[9])
    mat_copy.start()
    own_src = pltpu.make_async_copy(
        src.at[0, :, quarter_of(x, layer)], xin.at[mine, z, y, x], loc.at[0]
    )
    own_src.start()
    own_88 = pltpu.make_async_copy(src.at[0], own_rows, loc.at[1])
    own_88.start()
    own_green = []
    for c in range(N):
        to = green.at[mine, shift(z, c), x]
        for s, ref in ((0, gd), (1, gu)):
            @pl.when(sweep == s)
            def _(ref=ref, to=to, c=c):
                pltpu.make_async_copy(green_part(ref, c), to, loc.at[2 + c]).start()
        own_green.append(pltpu.make_async_copy(green_part(gd, c), to, loc.at[2 + c]))

    own_88.wait()
    pl.semaphore_wait(barrier, len(greet))

    def source_copy(dx, dl):
        to_x = shift(x, dx)
        to_l = layer if dl == 0 else sib
        rnd = (layer + to_x // 2) % 2
        return remote(
            own88.at[pl.ds(8, rows), quarter_of(to_x, to_l)], xin.at[rnd, z, y, x], src_s.at[dl, dx], src_r.at[dl, dx],
            device(to_l, z, y, to_x),
        )

    pairs = [(dx, dl) for dx in (2, 1, 3, 0) for dl in (0, 1) if (dx, dl) != (0, 0)]
    source_copies = {p: source_copy(*p) for p in pairs}
    for p in pairs:
        source_copies[p].start()

    mate = x + 1 - 2 * (x % 2)
    outer = lax.rem(x + N - 1 + 2 * (x % 2), N)
    far = shift(x, 2)
    OWN, MATE, OUTER, FAR = range(4)
    place = {OWN: x, MATE: mate, OUTER: outer, FAR: far}
    order = (0, 1, 3, 2)

    def to_mate(c, ref):
        return remote(
            green_part(ref, c), green.at[mine, shift(z, c), x],
            bulk_s.at[MATE, c], bulk_r.at[MATE, c], device(layer, z, y, mate),
        )

    def to_outer(c, ref):
        return remote(
            green_part(ref, c), green.at[1 - mine, shift(z, c), x],
            bulk_s.at[OUTER, c], bulk_r.at[OUTER, c], device(layer, z, y, outer),
        )

    def far_to_mate(c):
        at = green.at[mine, shift(z, c), outer]
        return remote(at, at, bulk_s.at[FAR, c], bulk_r.at[FAR, c], device(layer, z, y, mate))

    def to_sibling(kind, c, ref=None):
        at = green.at[mine, shift(z, c), place[kind]]
        return remote(
            at if ref is None else green_part(ref, c), at, fwd_s.at[kind, c], fwd_r.at[kind, c],
            device(sib, z, y, x),
        )

    def send_own(refs, other):
        for s, ref in ((0, refs[0]), (1, refs[1])):
            @pl.when(sweep == s)
            def _(ref=ref):
                for c in order:
                    (to_outer if other else to_mate)(c, ref).start()

    def own_to_sibling():
        for s, ref in ((0, gd), (1, gu)):
            @pl.when(sweep == s)
            def _(ref=ref):
                for c in order:
                    to_sibling(OWN, c, ref).start()

    def relay(c):
        to_outer(c, gd).wait_recv()
        far_to_mate(c).start()
        to_sibling(OUTER, c).start()

    @pl.when(mine == 0)
    def _():
        send_own((gd, gu), False)

    @pl.when(mine == 1)
    def _():
        send_own((gu, gd), True)

    own_to_sibling()

    other_copy = remote(own_rows, other, edge_s.at[2], edge_r.at[2], device(sib, z, y, x))
    other_copy.start()

    pml_copy.wait()
    mat_copy.wait()
    rows_at = lax.broadcasted_iota(jnp.int32, (rows, LANES), 0) + row * rows
    thick = jnp.full((rows, LANES), pml_s[0, 0].astype(F32))
    total = rows * N * N * N

    def ramp(index, count):
        dist = jnp.minimum(index, count - 1 - index).astype(F32)
        return jnp.maximum(thick - dist, 0.0) / thick

    ramp_m = ramp(rows_at, total)
    mt[...] = jnp.zeros_like(mt)
    mt[0:4, 0:rows] = 1.0 + 1.5 * mat_v[...].astype(F32)
    kappa = mt[...].T
    for k in range(4):
        ramp_z = ramp(jnp.full((rows, LANES), layer * 4 + k, jnp.int32), 8)
        sigma = 3.0 * (ramp_z * ramp_z + ramp_m * ramp_m)
        f = (4 - k) / 4
        around = (0 if k == 0 else (5 - k) / 4) + (0 if k == 3 else (3 - k) / 4)
        kap = jnp.broadcast_to(kappa[0:rows, k : k + 1], (rows, LANES))
        kc[k] = kap * (f * (4.0 + sigma) - around)
        kf[k] = kap * f
    res[:, 0:8] = jnp.zeros((2, 8, LANES), BF16)
    res[:, 4 * rows + 8 :] = jnp.zeros((2, 8, LANES), BF16)

    halves = (pl.ds(0, 2), pl.ds(2, 2))

    def plane_copy(rnd, part, from_z, from_y, sz, sy, to_z, to_y):
        at = xin.at[rnd, from_z, from_y, halves[part]]
        return remote(
            at, at, x_s.at[rnd, part, sz, sy], x_r.at[rnd, part, sz, sy],
            device(layer, to_z, to_y, x),
        )

    def first_stage(rnd):
        done = []
        for d in (2, 1, 3):
            done.append(plane_copy(rnd, 0, z, y, 0, d, z, shift(y, d)))
            done.append(plane_copy(rnd, 1, z, y, d, 0, shift(z, d), y))
        for d in (2, 1, 3):
            done.append(plane_copy(rnd, 0, z, y, d, 0, shift(z, d), y))
            done.append(plane_copy(rnd, 1, z, y, 0, d, z, shift(y, d)))
        for c in done:
            c.start()
        return done

    def arrival(rnd, part, sz, sy):
        from_z, from_y = shift(z, N - sz), shift(y, N - sy)
        at = xin.at[rnd, from_z, from_y, halves[part]]
        return remote(
            at, at, x_s.at[rnd, part, sz, sy], x_r.at[rnd, part, sz, sy], device(layer, z, y, x)
        )

    def second_stage(rnd):
        done = []
        for d in (1, 3, 2):
            if rnd == 0:
                @pl.when(mine == 0)
                def _(d=d):
                    relay(order[(0, 0, 2, 1)[d]])
            arrival(rnd, 0, 0, d).wait_recv()
            for q in (2, 1, 3):
                done.append(plane_copy(rnd, 0, z, shift(y, N - d), q, d, shift(z, q), y))
                done[-1].start()
            arrival(rnd, 1, d, 0).wait_recv()
            for q in (2, 1, 3):
                done.append(plane_copy(rnd, 1, shift(z, N - d), y, d, q, z, shift(y, q)))
                done[-1].start()
        return done

    def wait_plane(rnd, sz):
        for sy in (0, 1, 3, 2):
            for part in (0, 1):
                if (sz, sy) != (0, 0) and not (part == 0 and sz == 0) and not (part == 1 and sy == 0):
                    arrival(rnd, part, sz, sy).wait_recv()

    def wait_green(rnd, c):
        @pl.when(mine == rnd)
        def _():
            to_mate(c, gd).wait_recv()
            to_sibling(MATE, c).start()
            far_to_mate(c).wait_recv()
            to_sibling(FAR, c).start()
            own_green[c].wait()

        @pl.when(mine != rnd)
        def _():
            for kind in (OWN, OUTER, MATE, FAR):
                to_sibling(kind, c).wait_recv()

    def product(rnd):
        acc = None
        for c in order:
            wait_green(rnd, c)
            if rnd == 0 and c == order[1]:
                @pl.when(mine == 1)
                def _():
                    send_own((gd, gu), False)
            wait_plane(rnd, (N - c) % N)
            g = green[rnd, shift(z, c)].reshape(N * rows, chunk)
            v = xin[rnd, shift(z, c)].reshape(chunk, LANES)
            term = jnp.dot(g, v, preferred_element_type=F32)
            acc = term if acc is None else acc + term
        return acc.astype(BF16)

    def share(rnd):
        at_layer = sweep if rnd == 0 else 1 - sweep
        quarter = 2 * lax.rem(x, 2) + layer
        done = []
        for dx in (2, 1, 3, 0):
            to_x = shift(x, dx)
            at = res.at[rnd, pl.ds(pl.multiple_of(to_x * rows, 8), rows + 16)]
            to = fin.at[sweep, at_layer, quarter]
            for dl in (0, 1):
                if (dx, dl) == (0, 0):
                    done.append(pltpu.make_async_copy(at, to, loc.at[6 + rnd]))
                else:
                    done.append(remote(
                        at, to, fin_s.at[rnd, dl, dx], fin_r.at[rnd, dl, dx],
                        device(layer if dl == 0 else sib, z, y, to_x),
                    ))
        to = hal.at[sweep, quarter]
        up = remote(
            res.at[rnd, pl.ds(N * rows, 8)], to, hal_s.at[rnd, 0], hal_r.at[x, layer],
            (at_layer, lax.rem((group + 1) * N, N * N * N)),
        )
        down = remote(
            res.at[rnd, pl.ds(8, 8)], to, hal_s.at[rnd, 1], hal_r.at[x, layer],
            (at_layer, lax.rem(group * N + N * N * N - 1, N * N * N)),
        )
        return done, up, down

    def start_share(shared):
        done, up, down = shared

        @pl.when(group < N * N - 1)
        def _():
            up.start()

        @pl.when(group > 0)
        def _():
            down.start()

        for c in done:
            c.start()

    def sent_share(shared):
        done, up, down = shared

        @pl.when(group < N * N - 1)
        def _():
            up.wait_send()

        @pl.when(group > 0)
        def _():
            down.wait_send()

        for c in done[:-2] + done[-1:]:
            c.wait_send()

    def wait_sources(same_core):
        if same_core:
            own_src.wait()
        for p in pairs:
            if p[1] == (0 if same_core else 1):
                source_copies[p].wait_recv()

    for m in (0, 1):
        @pl.when(mine == m)
        def _(m=m):
            wait_sources(m == 0)
    sent = first_stage(0)
    sent += second_stage(0)

    @pl.when(mine == 0)
    def _():
        relay(order[3])
        send_own((gu, gd), True)

    res[0, 8 : N * rows + 8] = product(0)

    for m in (0, 1):
        @pl.when(mine == m)
        def _(m=m):
            wait_sources(m == 1)
    entry = xin[1, z, y].reshape(N * rows, LANES).astype(F32) + res[0, 8 : N * rows + 8].astype(F32)
    xin[1, z, y] = entry.astype(BF16).reshape(N, rows, LANES)
    sent2 = first_stage(1)
    shared = share(0)
    start_share(shared)

    edge_up = remote(
        own88.at[pl.ds(rows, 8)], own88.at[pl.ds(0, 8)], edge_s.at[0], edge_r.at[0],
        (layer, lax.rem(row + 1, N * N * N)),
    )
    edge_down = remote(
        own88.at[pl.ds(8, 8)], own88.at[pl.ds(rows + 8, 8)], edge_s.at[1], edge_r.at[1],
        (layer, lax.rem(row + N * N * N - 1, N * N * N)),
    )
    last = N * N * N - 1

    @pl.when(row < last)
    def _():
        edge_up.start()

    @pl.when(row > 0)
    def _():
        edge_down.start()


    @pl.when(mine == 1)
    def _():
        for c in order:
            relay(c)

    sent2 += second_stage(1)
    res[1, 8 : N * rows + 8] = product(1)
    shared2 = share(1)
    start_share(shared2)

    for c in sent + sent2:
        c.wait_send()
    for p in pairs:
        source_copies[p].wait_send()
    other_copy.wait()

    @pl.when(row < last)
    def _():
        edge_up.wait_send()
        edge_down.wait_recv()

    @pl.when(row > 0)
    def _():
        edge_down.wait_send()
        edge_up.wait_recv()

    sent_share(shared)
    for c in range(N):
        to_mate(c, gd).wait_send()
        to_outer(c, gd).wait_send()
        far_to_mate(c).wait_send()
        for kind in range(4):
            to_sibling(kind, c).wait_send()
    sent_share(shared2)

    for done, _, _ in (shared, shared2):
        done[-2].wait()
        for c in done[:-2] + done[-1:]:
            c.wait_recv()

    def wait_halo():
        for a in range(N):
            for b in range(2):
                remote(
                    res.at[0, pl.ds(0, 8)], hal.at[0, 0], hal_s.at[0, 0], hal_r.at[a, b],
                    device(sib, z, y, x),
                ).wait_recv()

    for q in range(4):
        cols = slice(q * LANES, (q + 1) * LANES)
        wave[:, cols] = (
            own88[:, cols].astype(F32) + fin[0, layer, q].astype(F32) + fin[1, layer, q].astype(F32)
        )

    def edge(at):
        wait_halo()
        for q in range(4):
            cols = slice(q * LANES, (q + 1) * LANES)
            wave[at : at + 8, cols] = (
                own88[at : at + 8, cols].astype(F32) + hal[0, q].astype(F32) + hal[1, q].astype(F32)
            )

    @pl.when(jnp.logical_and(x == 0, group > 0))
    def _():
        edge(0)

    @pl.when(jnp.logical_and(x == N - 1, group < N * N - 1))
    def _():
        edge(rows + 8)

    @pl.when(row == 0)
    def _():
        wave[0:8] = jnp.zeros((8, wave.shape[1]), F32)

    @pl.when(row == last)
    def _():
        wave[rows + 8 :] = jnp.zeros((8, wave.shape[1]), F32)

    here = layer.astype(F32)
    for q in range(4):
        cols = slice(q * LANES, (q + 1) * LANES)
        a = wave[8 : rows + 8, cols]
        b = wave[7 : rows + 7, cols] + wave[9 : rows + 9, cols]
        o = (
            other[:, cols].astype(F32)
            + fin[0, sib, q, 8 : rows + 8].astype(F32)
            + fin[1, sib, q, 8 : rows + 8].astype(F32)
        )
        for k in range(4):
            value = kc[k] * a - kf[k] * b
            if k == 0:
                value = value - kf[k] * (o * (0.25 * here))
            if k == 3:
                value = value - kf[k] * (o * (4.0 * (1.0 - here)))
            out[k, :, cols] = value.astype(BF16)


def local(source, green_down, green_up, material, pml_cells):
    rows, columns = source.shape[1:]
    points = green_down.shape[2]
    dma = pltpu.SemaphoreType.DMA
    hbm, vmem = pl.BlockSpec(memory_space=pltpu.HBM), pl.BlockSpec(memory_space=pltpu.VMEM)
    held = [
        pltpu.with_memory_space_constraint(v, pltpu.HBM)
        for v in (source, green_down, green_up, material)
    ]
    return pl.pallas_call(
        kernel,
        out_shape=jax.ShapeDtypeStruct((4, rows, columns), BF16),
        in_specs=[hbm] * 5,
        out_specs=vmem,
        scratch_shapes=[
            pltpu.SMEM((1, 1), jnp.int32),
            pltpu.VMEM((4, rows), jnp.int32),
            pltpu.VMEM((2, N, N, rows, points // N), BF16),
            pltpu.VMEM((2, N, N, N, rows, LANES), BF16),
            pltpu.VMEM((2, N * rows + 16, LANES), BF16),
            pltpu.VMEM((2, 2, 4, rows + 16, LANES), BF16),
            pltpu.VMEM((2, 4, 8, LANES), BF16),
            pltpu.VMEM((rows + 16, columns), BF16),
            pltpu.VMEM((rows, columns), BF16),
            pltpu.VMEM((rows + 16, columns), F32),
            pltpu.VMEM((4, rows, LANES), F32),
            pltpu.VMEM((4, rows, LANES), F32),
            pltpu.VMEM((8, LANES), F32),
            dma((N, N)), dma((N, N)), dma((N, N)), dma((N, N)),
            dma((2, N)), dma((2, N)),
            dma((2, 2, N, N)), dma((2, 2, N, N)),
            dma((2, 2, N)), dma((2, 2, N)),
            dma((2, 2)), dma((N, 2)),
            dma((3,)), dma((3,)),
            dma((10,)),
        ],
        compiler_params=pltpu.CompilerParams(
            collective_id=0, has_side_effects=True, vmem_limit_bytes=48 << 20
        ),
    )(*held, pml_cells.reshape(1, 1))


def solution(mesh):
    return jax.shard_map(
        local,
        mesh=mesh,
        in_specs=(
            P("layer", "row", None),
            P("layer", "row", None),
            P("layer", "row", None),
            P("layer", "row"),
            P(),
        ),
        out_specs=P("layer", "row", None),
        check_vma=False,
    )
```

```python
import functools

import jax
import jax.numpy as jnp
from jax import lax
from jax.experimental import pallas as pl
from jax.experimental.pallas import tpu as pltpu
from jax.sharding import PartitionSpec as P

MESH = pl.DeviceIdType.MESH
F32, BF16 = jnp.float32, jnp.bfloat16
N = 4
LANES = 128


def device(layer, z, y, x):
    return (layer, (z * N + y) * N + x)


def kernel(
    src, gd, gu, mat, pml, out,
    pml_s, mat_v, green, xin, res, fin, hal, own88, other, wave, kc, kf, mt,
    bulk_s, bulk_r, fwd_s, fwd_r, src_s, src_r, x_s, x_r, fin_s, fin_r,
    hal_s, hal_r, edge_s, edge_r, loc,
):
    layer = lax.axis_index("layer")
    row = lax.axis_index("row")
    z, y, x = row // (N * N), (row // N) % N, row % N
    group = z * N + y
    rows = src.shape[1]
    chunk = N * N * rows
    sweep = x // 2
    sib = 1 - layer
    mine = (layer + sweep) % 2

    def shift(a, d):
        return lax.rem(a + d, N)

    def remote(s, d, ss, rs, to):
        return pltpu.make_async_remote_copy(
            src_ref=s, dst_ref=d, send_sem=ss, recv_sem=rs, device_id=to, device_id_type=MESH
        )

    greet = [device(sib, z, y, x)]
    for d in (1, 2, 3):
        greet += [device(layer, z, y, shift(x, d)), device(sib, z, y, shift(x, d))]
        greet += [device(layer, z, shift(y, d), x), device(layer, shift(z, d), y, x)]
    barrier = pltpu.get_barrier_semaphore()
    for to in greet:
        pl.semaphore_signal(barrier, inc=1, device_id=to, device_id_type=MESH)

    def green_part(ref, c):
        return ref.at[0, :, pl.ds(pl.multiple_of(shift(z, c) * chunk, LANES), chunk)]

    own_rows = own88.at[pl.ds(8, rows)]

    def quarter_of(to_x, to_layer):
        return pl.ds(pl.multiple_of((2 * lax.rem(to_x, 2) + to_layer) * LANES, LANES), LANES)

    pml_copy = pltpu.make_async_copy(pml, pml_s, loc.at[8])
    pml_copy.start()
    mat_copy = pltpu.make_async_copy(mat, mat_v, loc.at[9])
    mat_copy.start()
    own_src = pltpu.make_async_copy(
        src.at[0, :, quarter_of(x, layer)], xin.at[mine, z, y, x], loc.at[0]
    )
    own_src.start()
    own_88 = pltpu.make_async_copy(src.at[0], own_rows, loc.at[1])
    own_88.start()
    own_green = []
    for c in range(N):
        to = green.at[mine, shift(z, c), x]
        for s, ref in ((0, gd), (1, gu)):
            @pl.when(sweep == s)
            def _(ref=ref, to=to, c=c):
                pltpu.make_async_copy(green_part(ref, c), to, loc.at[2 + c]).start()
        own_green.append(pltpu.make_async_copy(green_part(gd, c), to, loc.at[2 + c]))

    own_88.wait()
    pl.semaphore_wait(barrier, len(greet))

    def source_copy(dx, dl):
        to_x = shift(x, dx)
        to_l = layer if dl == 0 else sib
        rnd = (layer + to_x // 2) % 2
        return remote(
            own88.at[pl.ds(8, rows), quarter_of(to_x, to_l)], xin.at[rnd, z, y, x], src_s.at[dl, dx], src_r.at[dl, dx],
            device(to_l, z, y, to_x),
        )

    pairs = [(dx, dl) for dx in (2, 1, 3, 0) for dl in (0, 1) if (dx, dl) != (0, 0)]
    source_copies = {p: source_copy(*p) for p in pairs}
    for p in pairs:
        source_copies[p].start()

    mate = x + 1 - 2 * (x % 2)
    outer = lax.rem(x + N - 1 + 2 * (x % 2), N)
    far = shift(x, 2)
    OWN, MATE, OUTER, FAR = range(4)
    place = {OWN: x, MATE: mate, OUTER: outer, FAR: far}
    order = (0, 1, 3, 2)

    def to_mate(c, ref):
        return remote(
            green_part(ref, c), green.at[mine, shift(z, c), x],
            bulk_s.at[MATE, c], bulk_r.at[MATE, c], device(layer, z, y, mate),
        )

    def to_outer(c, ref):
        return remote(
            green_part(ref, c), green.at[1 - mine, shift(z, c), x],
            bulk_s.at[OUTER, c], bulk_r.at[OUTER, c], device(layer, z, y, outer),
        )

    def far_to_mate(c):
        at = green.at[mine, shift(z, c), outer]
        return remote(at, at, bulk_s.at[FAR, c], bulk_r.at[FAR, c], device(layer, z, y, mate))

    def to_sibling(kind, c, ref=None):
        at = green.at[mine, shift(z, c), place[kind]]
        return remote(
            at if ref is None else green_part(ref, c), at, fwd_s.at[kind, c], fwd_r.at[kind, c],
            device(sib, z, y, x),
        )

    def send_own(refs, other):
        for s, ref in ((0, refs[0]), (1, refs[1])):
            @pl.when(sweep == s)
            def _(ref=ref):
                for c in order:
                    (to_outer if other else to_mate)(c, ref).start()

    def own_to_sibling():
        for s, ref in ((0, gd), (1, gu)):
            @pl.when(sweep == s)
            def _(ref=ref):
                for c in order:
                    to_sibling(OWN, c, ref).start()

    def relay(c):
        to_outer(c, gd).wait_recv()
        far_to_mate(c).start()
        to_sibling(OUTER, c).start()

    @pl.when(mine == 0)
    def _():
        send_own((gd, gu), False)

    @pl.when(mine == 1)
    def _():
        send_own((gu, gd), True)

    own_to_sibling()

    other_copy = remote(own_rows, other, edge_s.at[2], edge_r.at[2], device(sib, z, y, x))
    other_copy.start()

    pml_copy.wait()
    mat_copy.wait()
    rows_at = lax.broadcasted_iota(jnp.int32, (rows, LANES), 0) + row * rows
    thick = jnp.full((rows, LANES), pml_s[0, 0].astype(F32))
    total = rows * N * N * N

    def ramp(index, count):
        dist = jnp.minimum(index, count - 1 - index).astype(F32)
        return jnp.maximum(thick - dist, 0.0) / thick

    ramp_m = ramp(rows_at, total)
    mt[...] = jnp.zeros_like(mt)
    mt[0:4, 0:rows] = 1.0 + 1.5 * mat_v[...].astype(F32)
    kappa = mt[...].T
    for k in range(4):
        ramp_z = ramp(jnp.full((rows, LANES), layer * 4 + k, jnp.int32), 8)
        sigma = 3.0 * (ramp_z * ramp_z + ramp_m * ramp_m)
        f = (4 - k) / 4
        around = (0 if k == 0 else (5 - k) / 4) + (0 if k == 3 else (3 - k) / 4)
        kap = jnp.broadcast_to(kappa[0:rows, k : k + 1], (rows, LANES))
        kc[k] = kap * (f * (4.0 + sigma) - around)
        kf[k] = kap * f
    res[:, 0:8] = jnp.zeros((2, 8, LANES), BF16)
    res[:, 4 * rows + 8 :] = jnp.zeros((2, 8, LANES), BF16)

    halves = (pl.ds(0, 2), pl.ds(2, 2))

    def plane_copy(rnd, part, from_z, from_y, sz, sy, to_z, to_y):
        at = xin.at[rnd, from_z, from_y, halves[part]]
        return remote(
            at, at, x_s.at[rnd, part, sz, sy], x_r.at[rnd, part, sz, sy],
            device(layer, to_z, to_y, x),
        )

    def first_stage(rnd):
        done = []
        for d in (2, 1, 3):
            done.append(plane_copy(rnd, 0, z, y, 0, d, z, shift(y, d)))
            done.append(plane_copy(rnd, 1, z, y, d, 0, shift(z, d), y))
        for d in (2, 1, 3):
            done.append(plane_copy(rnd, 0, z, y, d, 0, shift(z, d), y))
            done.append(plane_copy(rnd, 1, z, y, 0, d, z, shift(y, d)))
        for c in done:
            c.start()
        return done

    def arrival(rnd, part, sz, sy):
        from_z, from_y = shift(z, N - sz), shift(y, N - sy)
        at = xin.at[rnd, from_z, from_y, halves[part]]
        return remote(
            at, at, x_s.at[rnd, part, sz, sy], x_r.at[rnd, part, sz, sy], device(layer, z, y, x)
        )

    def second_stage(rnd):
        done = []
        for d in (1, 3, 2):
            if rnd == 0:
                @pl.when(mine == 0)
                def _(d=d):
                    relay(order[(0, 0, 2, 1)[d]])
            arrival(rnd, 0, 0, d).wait_recv()
            for q in (2, 1, 3):
                done.append(plane_copy(rnd, 0, z, shift(y, N - d), q, d, shift(z, q), y))
                done[-1].start()
            arrival(rnd, 1, d, 0).wait_recv()
            for q in (2, 1, 3):
                done.append(plane_copy(rnd, 1, shift(z, N - d), y, d, q, z, shift(y, q)))
                done[-1].start()
        return done

    def wait_plane(rnd, sz):
        for sy in (0, 1, 3, 2):
            for part in (0, 1):
                if (sz, sy) != (0, 0) and not (part == 0 and sz == 0) and not (part == 1 and sy == 0):
                    arrival(rnd, part, sz, sy).wait_recv()

    def wait_green(rnd, c):
        @pl.when(mine == rnd)
        def _():
            to_mate(c, gd).wait_recv()
            to_sibling(MATE, c).start()
            far_to_mate(c).wait_recv()
            to_sibling(FAR, c).start()
            own_green[c].wait()

        @pl.when(mine != rnd)
        def _():
            for kind in (OWN, OUTER, MATE, FAR):
                to_sibling(kind, c).wait_recv()

    def product(rnd):
        acc = None
        for c in order:
            wait_green(rnd, c)
            if rnd == 0 and c == order[1]:
                @pl.when(mine == 1)
                def _():
                    send_own((gd, gu), False)
            wait_plane(rnd, (N - c) % N)
            g = green[rnd, shift(z, c)].reshape(N * rows, chunk)
            v = xin[rnd, shift(z, c)].reshape(chunk, LANES)
            term = jnp.dot(g, v, preferred_element_type=F32)
            acc = term if acc is None else acc + term
        return acc.astype(BF16)

    def share(rnd):
        at_layer = sweep if rnd == 0 else 1 - sweep
        quarter = 2 * lax.rem(x, 2) + layer
        done = []
        for dx in (2, 1, 3, 0):
            to_x = shift(x, dx)
            at = res.at[rnd, pl.ds(pl.multiple_of(to_x * rows, 8), rows + 16)]
            to = fin.at[sweep, at_layer, quarter]
            for dl in (0, 1):
                if (dx, dl) == (0, 0):
                    done.append(pltpu.make_async_copy(at, to, loc.at[6 + rnd]))
                else:
                    done.append(remote(
                        at, to, fin_s.at[rnd, dl, dx], fin_r.at[rnd, dl, dx],
                        device(layer if dl == 0 else sib, z, y, to_x),
                    ))
        to = hal.at[sweep, quarter]
        up = remote(
            res.at[rnd, pl.ds(N * rows, 8)], to, hal_s.at[rnd, 0], hal_r.at[x, layer],
            (at_layer, lax.rem((group + 1) * N, N * N * N)),
        )
        down = remote(
            res.at[rnd, pl.ds(8, 8)], to, hal_s.at[rnd, 1], hal_r.at[x, layer],
            (at_layer, lax.rem(group * N + N * N * N - 1, N * N * N)),
        )
        return done, up, down

    def start_share(shared):
        done, up, down = shared

        @pl.when(group < N * N - 1)
        def _():
            up.start()

        @pl.when(group > 0)
        def _():
            down.start()

        for c in done:
            c.start()

    def sent_share(shared):
        done, up, down = shared

        @pl.when(group < N * N - 1)
        def _():
            up.wait_send()

        @pl.when(group > 0)
        def _():
            down.wait_send()

        for c in done[:-2] + done[-1:]:
            c.wait_send()

    def wait_sources(same_core):
        if same_core:
            own_src.wait()
        for p in pairs:
            if p[1] == (0 if same_core else 1):
                source_copies[p].wait_recv()

    for m in (0, 1):
        @pl.when(mine == m)
        def _(m=m):
            wait_sources(m == 0)
    sent = first_stage(0)
    sent += second_stage(0)

    @pl.when(mine == 0)
    def _():
        relay(order[3])
        send_own((gu, gd), True)

    res[0, 8 : N * rows + 8] = product(0)

    for m in (0, 1):
        @pl.when(mine == m)
        def _(m=m):
            wait_sources(m == 1)
    entry = xin[1, z, y].reshape(N * rows, LANES).astype(F32) + res[0, 8 : N * rows + 8].astype(F32)
    xin[1, z, y] = entry.astype(BF16).reshape(N, rows, LANES)
    sent2 = first_stage(1)
    shared = share(0)

    edge_up = remote(
        own88.at[pl.ds(rows, 8)], own88.at[pl.ds(0, 8)], edge_s.at[0], edge_r.at[0],
        (layer, lax.rem(row + 1, N * N * N)),
    )
    edge_down = remote(
        own88.at[pl.ds(8, 8)], own88.at[pl.ds(rows + 8, 8)], edge_s.at[1], edge_r.at[1],
        (layer, lax.rem(row + N * N * N - 1, N * N * N)),
    )
    last = N * N * N - 1

    @pl.when(row < last)
    def _():
        edge_up.start()

    @pl.when(row > 0)
    def _():
        edge_down.start()


    @pl.when(mine == 1)
    def _():
        for c in order:
            relay(c)

    sent2 += second_stage(1)
    start_share(shared)
    for c in sent:
        c.wait_send()
    for p in pairs:
        source_copies[p].wait_send()
    other_copy.wait()
    res[1, 8 : N * rows + 8] = product(1)
    shared2 = share(1)
    start_share(shared2)

    for c in sent2:
        c.wait_send()

    @pl.when(row < last)
    def _():
        edge_up.wait_send()
        edge_down.wait_recv()

    @pl.when(row > 0)
    def _():
        edge_down.wait_send()
        edge_up.wait_recv()

    sent_share(shared)
    for c in range(N):
        to_mate(c, gd).wait_send()
        to_outer(c, gd).wait_send()
        far_to_mate(c).wait_send()
        for kind in range(4):
            to_sibling(kind, c).wait_send()
    sent_share(shared2)

    for done, _, _ in (shared, shared2):
        done[-2].wait()
        for c in done[:-2] + done[-1:]:
            c.wait_recv()

    def wait_halo():
        for a in range(N):
            for b in range(2):
                remote(
                    res.at[0, pl.ds(0, 8)], hal.at[0, 0], hal_s.at[0, 0], hal_r.at[a, b],
                    device(sib, z, y, x),
                ).wait_recv()

    for q in range(4):
        cols = slice(q * LANES, (q + 1) * LANES)
        wave[:, cols] = (
            own88[:, cols].astype(F32) + fin[0, layer, q].astype(F32) + fin[1, layer, q].astype(F32)
        )

    def edge(at):
        wait_halo()
        for q in range(4):
            cols = slice(q * LANES, (q + 1) * LANES)
            wave[at : at + 8, cols] = (
                own88[at : at + 8, cols].astype(F32) + hal[0, q].astype(F32) + hal[1, q].astype(F32)
            )

    @pl.when(jnp.logical_and(x == 0, group > 0))
    def _():
        edge(0)

    @pl.when(jnp.logical_and(x == N - 1, group < N * N - 1))
    def _():
        edge(rows + 8)

    @pl.when(row == 0)
    def _():
        wave[0:8] = jnp.zeros((8, wave.shape[1]), F32)

    @pl.when(row == last)
    def _():
        wave[rows + 8 :] = jnp.zeros((8, wave.shape[1]), F32)

    here = layer.astype(F32)
    for q in range(4):
        cols = slice(q * LANES, (q + 1) * LANES)
        a = wave[8 : rows + 8, cols]
        b = wave[7 : rows + 7, cols] + wave[9 : rows + 9, cols]
        o = (
            other[:, cols].astype(F32)
            + fin[0, sib, q, 8 : rows + 8].astype(F32)
            + fin[1, sib, q, 8 : rows + 8].astype(F32)
        )
        for k in range(4):
            value = kc[k] * a - kf[k] * b
            if k == 0:
                value = value - kf[k] * (o * (0.25 * here))
            if k == 3:
                value = value - kf[k] * (o * (4.0 * (1.0 - here)))
            out[k, :, cols] = value.astype(BF16)


def local(source, green_down, green_up, material, pml_cells):
    rows, columns = source.shape[1:]
    points = green_down.shape[2]
    dma = pltpu.SemaphoreType.DMA
    hbm, vmem = pl.BlockSpec(memory_space=pltpu.HBM), pl.BlockSpec(memory_space=pltpu.VMEM)
    held = [
        pltpu.with_memory_space_constraint(v, pltpu.HBM)
        for v in (source, green_down, green_up, material)
    ]
    return pl.pallas_call(
        kernel,
        out_shape=jax.ShapeDtypeStruct((4, rows, columns), BF16),
        in_specs=[hbm] * 5,
        out_specs=vmem,
        scratch_shapes=[
            pltpu.SMEM((1, 1), jnp.int32),
            pltpu.VMEM((4, rows), jnp.int32),
            pltpu.VMEM((2, N, N, rows, points // N), BF16),
            pltpu.VMEM((2, N, N, N, rows, LANES), BF16),
            pltpu.VMEM((2, N * rows + 16, LANES), BF16),
            pltpu.VMEM((2, 2, 4, rows + 16, LANES), BF16),
            pltpu.VMEM((2, 4, 8, LANES), BF16),
            pltpu.VMEM((rows + 16, columns), BF16),
            pltpu.VMEM((rows, columns), BF16),
            pltpu.VMEM((rows + 16, columns), F32),
            pltpu.VMEM((4, rows, LANES), F32),
            pltpu.VMEM((4, rows, LANES), F32),
            pltpu.VMEM((8, LANES), F32),
            dma((N, N)), dma((N, N)), dma((N, N)), dma((N, N)),
            dma((2, N)), dma((2, N)),
            dma((2, 2, N, N)), dma((2, 2, N, N)),
            dma((2, 2, N)), dma((2, 2, N)),
            dma((2, 2)), dma((N, 2)),
            dma((3,)), dma((3,)),
            dma((10,)),
        ],
        compiler_params=pltpu.CompilerParams(
            collective_id=0, has_side_effects=True, vmem_limit_bytes=48 << 20
        ),
    )(*held, pml_cells.reshape(1, 1))


def solution(mesh):
    return jax.shard_map(
        local,
        mesh=mesh,
        in_specs=(
            P("layer", "row", None),
            P("layer", "row", None),
            P("layer", "row", None),
            P("layer", "row"),
            P(),
        ),
        out_specs=P("layer", "row", None),
        check_vma=False,
    )
```

```python
import functools

import jax
import jax.numpy as jnp
from jax import lax
from jax.experimental import pallas as pl
from jax.experimental.pallas import tpu as pltpu
from jax.sharding import PartitionSpec as P

MESH = pl.DeviceIdType.MESH
F32, BF16 = jnp.float32, jnp.bfloat16
N = 4
LANES = 128


def device(layer, z, y, x):
    return (layer, (z * N + y) * N + x)


def kernel(
    src, gd, gu, mat, pml, out,
    pml_s, mat_v, green, xin, res, fin, hal, own88, other, across, wave, kc, kf, mt,
    bulk_s, bulk_r, fwd_s, fwd_r, src_s, src_r, x_s, x_r, fin_s, fin_r,
    hal_s, hal_r, edge_s, edge_r, loc,
):
    layer = lax.axis_index("layer")
    row = lax.axis_index("row")
    z, y, x = row // (N * N), (row // N) % N, row % N
    group = z * N + y
    rows = src.shape[1]
    chunk = N * N * rows
    sweep = x // 2
    sib = 1 - layer
    mine = (layer + sweep) % 2

    def shift(a, d):
        return lax.rem(a + d, N)

    def remote(s, d, ss, rs, to):
        return pltpu.make_async_remote_copy(
            src_ref=s, dst_ref=d, send_sem=ss, recv_sem=rs, device_id=to, device_id_type=MESH
        )

    greet = [device(sib, z, y, x)]
    for d in (1, 2, 3):
        greet += [device(layer, z, y, shift(x, d)), device(sib, z, y, shift(x, d))]
        greet += [device(layer, z, shift(y, d), x), device(layer, shift(z, d), y, x)]
    barrier = pltpu.get_barrier_semaphore()
    for to in greet:
        pl.semaphore_signal(barrier, inc=1, device_id=to, device_id_type=MESH)

    def green_part(ref, c):
        return ref.at[0, :, pl.ds(pl.multiple_of(shift(z, c) * chunk, LANES), chunk)]

    own_rows = own88.at[pl.ds(8, rows)]

    def quarter_of(to_x, to_layer):
        return pl.ds(pl.multiple_of((2 * lax.rem(to_x, 2) + to_layer) * LANES, LANES), LANES)

    pml_copy = pltpu.make_async_copy(pml, pml_s, loc.at[8])
    pml_copy.start()
    mat_copy = pltpu.make_async_copy(mat, mat_v, loc.at[9])
    mat_copy.start()
    own_src = pltpu.make_async_copy(
        src.at[0, :, quarter_of(x, layer)], xin.at[mine, z, y, x], loc.at[0]
    )
    own_src.start()
    own_88 = pltpu.make_async_copy(src.at[0], own_rows, loc.at[1])
    own_88.start()
    own_green = []
    for c in range(N):
        to = green.at[mine, shift(z, c), x]
        for s, ref in ((0, gd), (1, gu)):
            @pl.when(sweep == s)
            def _(ref=ref, to=to, c=c):
                pltpu.make_async_copy(green_part(ref, c), to, loc.at[2 + c]).start()
        own_green.append(pltpu.make_async_copy(green_part(gd, c), to, loc.at[2 + c]))

    own_88.wait()
    pl.semaphore_wait(barrier, len(greet))

    def source_copy(dx, dl):
        to_x = shift(x, dx)
        to_l = layer if dl == 0 else sib
        rnd = (layer + to_x // 2) % 2
        return remote(
            own88.at[pl.ds(8, rows), quarter_of(to_x, to_l)], xin.at[rnd, z, y, x], src_s.at[dl, dx], src_r.at[dl, dx],
            device(to_l, z, y, to_x),
        )

    pairs = [(dx, dl) for dx in (2, 1, 3, 0) for dl in (0, 1) if (dx, dl) != (0, 0)]
    source_copies = {p: source_copy(*p) for p in pairs}
    for p in pairs:
        source_copies[p].start()

    mate = x + 1 - 2 * (x % 2)
    outer = lax.rem(x + N - 1 + 2 * (x % 2), N)
    far = shift(x, 2)
    OWN, MATE, OUTER, FAR = range(4)
    place = {OWN: x, MATE: mate, OUTER: outer, FAR: far}
    order = (0, 1, 3, 2)

    def to_mate(c, ref):
        return remote(
            green_part(ref, c), green.at[mine, shift(z, c), x],
            bulk_s.at[MATE, c], bulk_r.at[MATE, c], device(layer, z, y, mate),
        )

    def to_outer(c, ref):
        return remote(
            green_part(ref, c), green.at[1 - mine, shift(z, c), x],
            bulk_s.at[OUTER, c], bulk_r.at[OUTER, c], device(layer, z, y, outer),
        )

    def far_to_mate(c):
        at = green.at[mine, shift(z, c), outer]
        return remote(at, at, bulk_s.at[FAR, c], bulk_r.at[FAR, c], device(layer, z, y, mate))

    def to_sibling(kind, c, ref=None):
        at = green.at[mine, shift(z, c), place[kind]]
        return remote(
            at if ref is None else green_part(ref, c), at, fwd_s.at[kind, c], fwd_r.at[kind, c],
            device(sib, z, y, x),
        )

    def send_own(refs, other):
        for s, ref in ((0, refs[0]), (1, refs[1])):
            @pl.when(sweep == s)
            def _(ref=ref):
                for c in order:
                    (to_outer if other else to_mate)(c, ref).start()

    def own_to_sibling():
        for s, ref in ((0, gd), (1, gu)):
            @pl.when(sweep == s)
            def _(ref=ref):
                for c in order:
                    to_sibling(OWN, c, ref).start()

    def relay(c):
        to_outer(c, gd).wait_recv()
        far_to_mate(c).start()
        to_sibling(OUTER, c).start()

    @pl.when(mine == 0)
    def _():
        send_own((gd, gu), False)

    @pl.when(mine == 1)
    def _():
        send_own((gu, gd), True)

    own_to_sibling()

    other_copy = remote(own_rows, other, edge_s.at[2], edge_r.at[2], device(sib, z, y, x))
    other_copy.start()

    pml_copy.wait()
    mat_copy.wait()
    rows_at = lax.broadcasted_iota(jnp.int32, (rows, LANES), 0) + row * rows
    thick = jnp.full((rows, LANES), pml_s[0, 0].astype(F32))
    total = rows * N * N * N

    def ramp(index, count):
        dist = jnp.minimum(index, count - 1 - index).astype(F32)
        return jnp.maximum(thick - dist, 0.0) / thick

    ramp_m = ramp(rows_at, total)
    mt[...] = jnp.zeros_like(mt)
    mt[0:4, 0:rows] = 1.0 + 1.5 * mat_v[...].astype(F32)
    kappa = mt[...].T
    for k in range(4):
        ramp_z = ramp(jnp.full((rows, LANES), layer * 4 + k, jnp.int32), 8)
        sigma = 3.0 * (ramp_z * ramp_z + ramp_m * ramp_m)
        f = (4 - k) / 4
        around = (0 if k == 0 else (5 - k) / 4) + (0 if k == 3 else (3 - k) / 4)
        kap = jnp.broadcast_to(kappa[0:rows, k : k + 1], (rows, LANES))
        kc[k] = kap * (f * (4.0 + sigma) - around)
        kf[k] = kap * f
    res[:, 0:8] = jnp.zeros((2, 8, LANES), BF16)
    res[:, 4 * rows + 8 :] = jnp.zeros((2, 8, LANES), BF16)

    halves = (pl.ds(0, 2), pl.ds(2, 2))

    def plane_copy(rnd, part, from_z, from_y, sz, sy, to_z, to_y):
        at = xin.at[rnd, from_z, from_y, halves[part]]
        return remote(
            at, at, x_s.at[rnd, part, sz, sy], x_r.at[rnd, part, sz, sy],
            device(layer, to_z, to_y, x),
        )

    def first_stage(rnd):
        done = []
        for d in (2, 1, 3):
            done.append(plane_copy(rnd, 0, z, y, 0, d, z, shift(y, d)))
            done.append(plane_copy(rnd, 1, z, y, d, 0, shift(z, d), y))
        for d in (2, 1, 3):
            done.append(plane_copy(rnd, 0, z, y, d, 0, shift(z, d), y))
            done.append(plane_copy(rnd, 1, z, y, 0, d, z, shift(y, d)))
        for c in done:
            c.start()
        return done

    def arrival(rnd, part, sz, sy):
        from_z, from_y = shift(z, N - sz), shift(y, N - sy)
        at = xin.at[rnd, from_z, from_y, halves[part]]
        return remote(
            at, at, x_s.at[rnd, part, sz, sy], x_r.at[rnd, part, sz, sy], device(layer, z, y, x)
        )

    def second_stage(rnd):
        done = []
        for d in (1, 3, 2):
            if rnd == 0:
                @pl.when(mine == 0)
                def _(d=d):
                    relay(order[(0, 0, 2, 1)[d]])
            arrival(rnd, 0, 0, d).wait_recv()
            for q in (2, 1, 3):
                done.append(plane_copy(rnd, 0, z, shift(y, N - d), q, d, shift(z, q), y))
                done[-1].start()
            arrival(rnd, 1, d, 0).wait_recv()
            for q in (2, 1, 3):
                done.append(plane_copy(rnd, 1, shift(z, N - d), y, d, q, z, shift(y, q)))
                done[-1].start()
        return done

    def wait_plane(rnd, sz):
        for sy in (0, 1, 3, 2):
            for part in (0, 1):
                if (sz, sy) != (0, 0) and not (part == 0 and sz == 0) and not (part == 1 and sy == 0):
                    arrival(rnd, part, sz, sy).wait_recv()

    def wait_green(rnd, c):
        @pl.when(mine == rnd)
        def _():
            to_mate(c, gd).wait_recv()
            to_sibling(MATE, c).start()
            far_to_mate(c).wait_recv()
            to_sibling(FAR, c).start()
            own_green[c].wait()

        @pl.when(mine != rnd)
        def _():
            for kind in (OWN, OUTER, MATE, FAR):
                to_sibling(kind, c).wait_recv()

    def product(rnd, idle=None):
        acc = None
        for c in order:
            if idle is not None and c == order[3]:
                idle()
            wait_green(rnd, c)
            if rnd == 0 and c == order[1]:
                @pl.when(mine == 1)
                def _():
                    send_own((gd, gu), False)
            wait_plane(rnd, (N - c) % N)
            g = green[rnd, shift(z, c)].reshape(N * rows, chunk)
            v = xin[rnd, shift(z, c)].reshape(chunk, LANES)
            term = jnp.dot(g, v, preferred_element_type=F32)
            acc = term if acc is None else acc + term
        return acc.astype(BF16)

    def share(rnd):
        at_layer = sweep if rnd == 0 else 1 - sweep
        quarter = 2 * lax.rem(x, 2) + layer
        done = []
        for dx in (2, 1, 3, 0):
            to_x = shift(x, dx)
            at = res.at[rnd, pl.ds(pl.multiple_of(to_x * rows, 8), rows + 16)]
            to = fin.at[sweep, at_layer, quarter]
            for dl in (0, 1):
                if (dx, dl) == (0, 0):
                    done.append(pltpu.make_async_copy(at, to, loc.at[6 + rnd]))
                else:
                    done.append(remote(
                        at, to, fin_s.at[rnd, dl, dx], fin_r.at[rnd, dl, dx],
                        device(layer if dl == 0 else sib, z, y, to_x),
                    ))
        to = hal.at[sweep, quarter]
        up = remote(
            res.at[rnd, pl.ds(N * rows, 8)], to, hal_s.at[rnd, 0], hal_r.at[x, layer],
            (at_layer, lax.rem((group + 1) * N, N * N * N)),
        )
        down = remote(
            res.at[rnd, pl.ds(8, 8)], to, hal_s.at[rnd, 1], hal_r.at[x, layer],
            (at_layer, lax.rem(group * N + N * N * N - 1, N * N * N)),
        )
        return done, up, down

    def start_share(shared):
        done, up, down = shared

        @pl.when(group < N * N - 1)
        def _():
            up.start()

        @pl.when(group > 0)
        def _():
            down.start()

        for c in done:
            c.start()

    def sent_share(shared):
        done, up, down = shared

        @pl.when(group < N * N - 1)
        def _():
            up.wait_send()

        @pl.when(group > 0)
        def _():
            down.wait_send()

        for c in done[:-2] + done[-1:]:
            c.wait_send()

    def wait_sources(same_core):
        if same_core:
            own_src.wait()
        for p in pairs:
            if p[1] == (0 if same_core else 1):
                source_copies[p].wait_recv()

    for m in (0, 1):
        @pl.when(mine == m)
        def _(m=m):
            wait_sources(m == 0)
    sent = first_stage(0)
    sent += second_stage(0)

    @pl.when(mine == 0)
    def _():
        relay(order[3])
        send_own((gu, gd), True)

    res[0, 8 : N * rows + 8] = product(0)

    for m in (0, 1):
        @pl.when(mine == m)
        def _(m=m):
            wait_sources(m == 1)
    entry = xin[1, z, y].reshape(N * rows, LANES).astype(F32) + res[0, 8 : N * rows + 8].astype(F32)
    xin[1, z, y] = entry.astype(BF16).reshape(N, rows, LANES)
    sent2 = first_stage(1)
    shared = share(0)

    edge_up = remote(
        own88.at[pl.ds(rows, 8)], own88.at[pl.ds(0, 8)], edge_s.at[0], edge_r.at[0],
        (layer, lax.rem(row + 1, N * N * N)),
    )
    edge_down = remote(
        own88.at[pl.ds(8, 8)], own88.at[pl.ds(rows + 8, 8)], edge_s.at[1], edge_r.at[1],
        (layer, lax.rem(row + N * N * N - 1, N * N * N)),
    )
    last = N * N * N - 1

    @pl.when(row < last)
    def _():
        edge_up.start()

    @pl.when(row > 0)
    def _():
        edge_down.start()


    @pl.when(mine == 1)
    def _():
        for c in order:
            relay(c)

    sent2 += second_stage(1)
    start_share(shared)
    for c in sent:
        c.wait_send()
    for p in pairs:
        source_copies[p].wait_send()
    other_copy.wait()
    def sent_before():
        for c in sent2:
            c.wait_send()
        for c in range(N):
            to_outer(c, gd).wait_send()
            to_sibling(OWN, c).wait_send()

    res[1, 8 : N * rows + 8] = product(1, sent_before)
    shared2 = share(1)
    start_share(shared2)

    @pl.when(row < last)
    def _():
        edge_up.wait_send()
        edge_down.wait_recv()

    @pl.when(row > 0)
    def _():
        edge_down.wait_send()
        edge_up.wait_recv()

    sent_share(shared)
    for c in range(N):
        to_mate(c, gd).wait_send()
        far_to_mate(c).wait_send()
        for kind in (MATE, OUTER, FAR):
            to_sibling(kind, c).wait_send()
    sent_share(shared2)

    def wait_share(done):
        done[-2].wait()
        for c in done[:-2] + done[-1:]:
            c.wait_recv()

    wait_share(shared[0])
    for q in range(4):
        cols = slice(q * LANES, (q + 1) * LANES)
        wave[:, cols] = own88[:, cols].astype(F32) + fin[layer, layer, q].astype(F32)
        across[:, cols] = other[:, cols].astype(F32) + fin[sib, sib, q, 8 : rows + 8].astype(F32)
    wait_share(shared2[0])

    def wait_halo():
        for a in range(N):
            for b in range(2):
                remote(
                    res.at[0, pl.ds(0, 8)], hal.at[0, 0], hal_s.at[0, 0], hal_r.at[a, b],
                    device(sib, z, y, x),
                ).wait_recv()

    for q in range(4):
        cols = slice(q * LANES, (q + 1) * LANES)
        wave[:, cols] = wave[:, cols] + fin[sib, layer, q].astype(F32)

    def edge(at):
        wait_halo()
        for q in range(4):
            cols = slice(q * LANES, (q + 1) * LANES)
            wave[at : at + 8, cols] = (
                own88[at : at + 8, cols].astype(F32) + hal[0, q].astype(F32) + hal[1, q].astype(F32)
            )

    @pl.when(jnp.logical_and(x == 0, group > 0))
    def _():
        edge(0)

    @pl.when(jnp.logical_and(x == N - 1, group < N * N - 1))
    def _():
        edge(rows + 8)

    @pl.when(row == 0)
    def _():
        wave[0:8] = jnp.zeros((8, wave.shape[1]), F32)

    @pl.when(row == last)
    def _():
        wave[rows + 8 :] = jnp.zeros((8, wave.shape[1]), F32)

    here = layer.astype(F32)
    for q in range(4):
        cols = slice(q * LANES, (q + 1) * LANES)
        a = wave[8 : rows + 8, cols]
        b = wave[7 : rows + 7, cols] + wave[9 : rows + 9, cols]
        o = across[:, cols] + fin[layer, sib, q, 8 : rows + 8].astype(F32)
        for k in range(4):
            value = kc[k] * a - kf[k] * b
            if k == 0:
                value = value - kf[k] * (o * (0.25 * here))
            if k == 3:
                value = value - kf[k] * (o * (4.0 * (1.0 - here)))
            out[k, :, cols] = value.astype(BF16)


def local(source, green_down, green_up, material, pml_cells):
    rows, columns = source.shape[1:]
    points = green_down.shape[2]
    dma = pltpu.SemaphoreType.DMA
    hbm, vmem = pl.BlockSpec(memory_space=pltpu.HBM), pl.BlockSpec(memory_space=pltpu.VMEM)
    held = [
        pltpu.with_memory_space_constraint(v, pltpu.HBM)
        for v in (source, green_down, green_up, material)
    ]
    return pl.pallas_call(
        kernel,
        out_shape=jax.ShapeDtypeStruct((4, rows, columns), BF16),
        in_specs=[hbm] * 5,
        out_specs=vmem,
        scratch_shapes=[
            pltpu.SMEM((1, 1), jnp.int32),
            pltpu.VMEM((4, rows), jnp.int32),
            pltpu.VMEM((2, N, N, rows, points // N), BF16),
            pltpu.VMEM((2, N, N, N, rows, LANES), BF16),
            pltpu.VMEM((2, N * rows + 16, LANES), BF16),
            pltpu.VMEM((2, 2, 4, rows + 16, LANES), BF16),
            pltpu.VMEM((2, 4, 8, LANES), BF16),
            pltpu.VMEM((rows + 16, columns), BF16),
            pltpu.VMEM((rows, columns), BF16),
            pltpu.VMEM((rows, columns), F32),
            pltpu.VMEM((rows + 16, columns), F32),
            pltpu.VMEM((4, rows, LANES), F32),
            pltpu.VMEM((4, rows, LANES), F32),
            pltpu.VMEM((8, LANES), F32),
            dma((N, N)), dma((N, N)), dma((N, N)), dma((N, N)),
            dma((2, N)), dma((2, N)),
            dma((2, 2, N, N)), dma((2, 2, N, N)),
            dma((2, 2, N)), dma((2, 2, N)),
            dma((2, 2)), dma((N, 2)),
            dma((3,)), dma((3,)),
            dma((10,)),
        ],
        compiler_params=pltpu.CompilerParams(
            collective_id=0, has_side_effects=True, vmem_limit_bytes=48 << 20
        ),
    )(*held, pml_cells.reshape(1, 1))


def solution(mesh):
    return jax.shard_map(
        local,
        mesh=mesh,
        in_specs=(
            P("layer", "row", None),
            P("layer", "row", None),
            P("layer", "row", None),
            P("layer", "row"),
            P(),
        ),
        out_specs=P("layer", "row", None),
        check_vma=False,
    )
```
